32 devices in a mesh: dom: 8 (over y, x, core), cls: 4 (over z).
Axes of the slice: x: 2, y: 2, z: 4, core: 2. Of those that a mesh axis runs over, the one named last changes fastest.
Arguments:
- particles: bfloat16 [4096, 9216], P(('dom', 'cls')), may hold values from -6 to 6
- references: bfloat16 [200, 9216], P('cls', 'dom'), may hold values from -0.0625 to 0.0625
- owner: int32 [4096, 1], P(('dom', 'cls')), may hold values from 0 to 3; in each aligned block of 128 rows (0 to 127, 128 to 255, ...) at most 64 rows name the same one
- class_offset: int32 [4096], P(('dom', 'cls')), may hold values from 0 to 49
- rotation: int32 [4096], P(('dom', 'cls')), may hold values from 0 to 71
- shifts: int32 [4096, 2], P(('dom', 'cls')), may hold values from -6 to 6
- ctf_group: int32 [4096], P(('dom', 'cls')), may hold values from 0 to 63, as said below
- ctf_table: float32 [64, 64], replicated, may hold values from -6 to 6
Outputs:
- best_score: float32 [4096], P(('dom', 'cls'))
- new_references: float32 [200, 9216], P('cls', 'dom')
The draws below stay inside these ranges and needn't reach their ends.
Inputs may be any that keep to these rules, and one draw needn't show every extreme that they name: Among the particles of one device no owner index is named more than 64 times, a bound that some block reaches. `ctf_group`: the particles of device block i (rows i * 128 to (i + 1) * 128 - 1) use only groups i * 2 to (i + 1) * 2 - 1.
All inputs are finite; a program needn't handle non-finite values.
Results may differ from the reference program's by a relative error of at most 0.0029.
Values may be sent and summed in bfloat16 or wider, within the bound.
A program may use at most 128 MiB of HBM per device.

```python
import math
import jax
import jax.numpy as jnp
import numpy as np
from jax import lax

A = 72
R = 64
CLASSES = 200
BOX = 128
SHIFT = 6
GPD = 2
P_DEV = 128
P_ALL = 4096
CPD = 50
CAP = 64
GROUPS = 64
N_CLS = 4


def draw_ctf_group(key, part):
    first_rows = jnp.arange(P_ALL, dtype=jnp.int32) // P_DEV * GPD
    return first_rows + jax.random.randint(key, (P_ALL,), 0, GPD, dtype=jnp.int32)


def draw_ctf_table(key, part):
    level = jnp.arange(GROUPS, dtype=jnp.float32) / (GROUPS - 1)
    scale_rows = 10.0 ** (0.5 * level)
    values_out = jnp.clip(0.6 * jax.random.normal(key, (GROUPS, R), jnp.float32), -1.0, 1.0)
    return values_out * scale_rows[:, None]


def with_ends(result, rng, low, top_value):
    longest = result.shape.index(max(result.shape))
    spots = []
    for shift in (0, 1):
        where = [jax.random.randint(jax.random.fold_in(rng, axis), (), 0, length) for axis, length in enumerate(result.shape)]
        where[longest] = (where[longest] + shift) % result.shape[longest]
        spots.append(tuple(where))
    return result.at[spots[0]].set(low).at[spots[1]].set(top_value)


def block_levels(own_key, dims, cuts, low, largest):
    gain = 1.0
    for position, shards_of in cuts:
        draws = jax.random.uniform(jax.random.fold_in(jax.random.fold_in(own_key, 6), position), (shards_of,), jnp.float32, low / len(cuts), largest / len(cuts))
        gain = gain * jnp.repeat(jnp.exp(draws), dims[position] // shards_of).reshape((-1,) + (1,) * (len(dims) - 1 - position))
    return gain


def shared_out(key, own, number, rows, count, top, limit, lean):
    order = jax.random.permutation(key, count)
    crowded, usual = load_shares(count, rows * top, limit, lean, True), load_shares(count, rows * top, limit, lean, False)
    places = jnp.arange(count)

    def named(tallies, turn):
        used = int((tallies > 0).sum())
        fixed = max(1, used // 4)
        moved = fixed + (places - fixed + turn * (used - fixed)) % max(1, count - fixed)
        return jnp.zeros((count,), jnp.int32).at[order[jnp.where(places < fixed, places, moved)]].set(jnp.asarray(tallies, jnp.int32))

    tallies = jnp.where(number % 4 == 0, named(crowded, number // 4), named(usual, number - number // 4 - 1))
    mixed = jax.random.permutation(jax.random.fold_in(own, 3), count)
    giver, taker = mixed[0:count // 2 * 2:2], mixed[1:count // 2 * 2:2]
    slack = jnp.minimum(tallies[giver] - 1, limit - tallies[taker]) // 2
    slack = jnp.where((giver == order[0]) | (taker == order[0]) | (tallies[taker] == 0), 0, jnp.maximum(slack, 0))
    moved = jax.random.randint(jax.random.fold_in(own, 4), (count // 2,), 0, 1 << 20) % (slack + 1)
    tallies = tallies.at[giver].add(-moved).at[taker].add(moved)
    items = jnp.searchsorted(jnp.cumsum(tallies), jnp.arange(rows * top), side="right").astype(jnp.int32)
    grid = items.reshape(top, rows).T
    grid = grid[jax.random.permutation(jax.random.fold_in(own, 1), rows)]
    turn = jax.random.randint(jax.random.fold_in(own, 2), (rows, 1), 0, top)
    return jnp.take_along_axis(grid, (jnp.arange(top)[None, :] + turn) % top, axis=1)


def load_shares(count, total, bound, lean, full):
    weights = [(1 << 20) // math.isqrt(grade ** lean) + 1 for grade in range(1, count + 1)]
    largest = bound if full else min(bound, max(-(-total // count), total * weights[0] // sum(weights)))
    least = 1 if total - largest >= count - 1 else 0
    given, spare = [largest] + [least] * (count - 1), total - largest - least * (count - 1)
    while spare > 0:
        movable = [i for i in range(1, count) if given[i] < largest] or [i for i in range(1, count) if given[i] < bound]
        pool, left = sum([weights[i] for i in movable]), spare
        for i in movable:
            addition = min(bound - given[i], max(1, left * weights[i] // pool), spare)
            given[i] = given[i] + addition
            spare = spare - addition
    return np.array(given)


def centred(stream_key, shape, spread, most, shards=(), kind=jnp.bfloat16):
    drawn = spread * jax.random.normal(stream_key, shape, jnp.float32)
    if shards:
        drawn = drawn * block_levels(stream_key, shape, shards, -0.22, 0.18)
    return jnp.clip(drawn, -most, most).astype(kind)


def setup_inputs(seed: int = 0) -> dict:
    arg_keys = jax.random.split(jax.random.key(seed), 9)
    particles = centred(arg_keys[0], (P_ALL, 2 * A * R), 1.0, 6.0, ((0, 32),))
    references = centred(arg_keys[1], (CLASSES, 2 * A * R), (2 * A * R) ** -0.5, 0.0625, ((0, 4), (1, 8)))
    owner_keys = jax.random.split(jax.random.fold_in(arg_keys[2], 1), P_ALL // P_DEV)
    owner_turns = jax.random.permutation(jax.random.fold_in(arg_keys[2], 3), P_ALL // P_DEV)
    owner = jax.vmap(lambda own, number: shared_out(jax.random.fold_in(arg_keys[2], 2), own, number, P_DEV, N_CLS, 1, CAP, 1))(owner_keys, owner_turns).reshape((P_ALL, 1))
    class_offset = with_ends(jax.random.randint(arg_keys[3], (P_ALL,), 0, CPD), jax.random.fold_in(arg_keys[3], 1), 0, CPD - 1).astype(jnp.int32)
    rotation = with_ends(jax.random.randint(arg_keys[4], (P_ALL,), 0, A), jax.random.fold_in(arg_keys[4], 1), 0, A - 1).astype(jnp.int32)
    shifts = with_ends(jax.random.randint(arg_keys[5], (P_ALL, 2), 0 - SHIFT, SHIFT + 1), jax.random.fold_in(arg_keys[5], 1), 0 - SHIFT, SHIFT).astype(jnp.int32)
    ctf_group = draw_ctf_group(jax.random.fold_in(arg_keys[8], 71), 0)
    ctf_table = draw_ctf_table(jax.random.fold_in(arg_keys[8], 71), 0)
    return {"particles": particles, "references": references, "owner": owner, "class_offset": class_offset, "rotation": rotation, "shifts": shifts, "ctf_group": ctf_group, "ctf_table": ctf_table}


tau_reg = 1.0


def angle_tables(angles):
    index_grid = (jnp.arange(angles, dtype=jnp.int32)[:, None] * jnp.arange(angles, dtype=jnp.int32)[None, :]) % angles
    turn_grid = 2.0 * math.pi * index_grid.astype(jnp.float32) / angles
    cosine = jnp.cos(turn_grid)
    sine_part = jnp.sin(turn_grid)
    forward = jnp.concatenate([cosine, -sine_part], axis=0).astype(jnp.bfloat16)
    inverse = (jnp.concatenate([cosine, -sine_part], axis=1) / angles).astype(jnp.bfloat16)
    return forward, inverse


def prepare(particle_rows, shift_rows, group_rows, ctf_table):
    count_rows = particle_rows.shape[0]
    cycle_count = ctf_table.shape[1]
    angles = particle_rows.shape[1] // (2 * cycle_count)
    values_in = particle_rows.reshape(count_rows, angles, 2, cycle_count).astype(jnp.float32)
    angle_grid = 2.0 * math.pi * jnp.arange(angles, dtype=jnp.float32) / angles
    radius = jnp.arange(1, cycle_count + 1, dtype=jnp.float32)
    freq_x = jnp.cos(angle_grid)[:, None] * radius[None, :]
    freq_y = jnp.sin(angle_grid)[:, None] * radius[None, :]
    move_x = shift_rows[:, 0].astype(jnp.float32)[:, None, None]
    move_y = shift_rows[:, 1].astype(jnp.float32)[:, None, None]
    phase_grid = 2.0 * math.pi * (move_x * freq_x[None] + move_y * freq_y[None]) / BOX
    cosine = jnp.cos(phase_grid)
    sine_part = jnp.sin(phase_grid)
    selector = (group_rows[:, None] == jnp.arange(ctf_table.shape[0], dtype=jnp.int32)[None, :]).astype(jnp.float32)
    ctf_rows = jnp.dot(selector, ctf_table, precision=lax.Precision.HIGHEST, preferred_element_type=jnp.float32)
    real_in = values_in[:, :, 0, :]
    imag_in = values_in[:, :, 1, :]
    real_out = (real_in * cosine - imag_in * sine_part) * ctf_rows[:, None, :]
    imag_out = (real_in * sine_part + imag_in * cosine) * ctf_rows[:, None, :]
    weighted = jnp.stack([real_out, imag_out], axis=2).reshape(count_rows, angles * 2 * cycle_count)
    return weighted.astype(jnp.bfloat16), ctf_rows


def spectra_of(flat_rows, forward, cycle_count):
    angles = forward.shape[1]
    shaped = flat_rows.reshape(flat_rows.shape[0], angles, 2 * cycle_count)
    spectra = jnp.einsum('ja,nac->jnc', forward.astype(jnp.float32), shaped.astype(jnp.float32),
                         precision=lax.Precision.HIGHEST).astype(jnp.bfloat16)
    return jnp.concatenate([spectra[:angles], spectra[angles:]], axis=2)


def paired(ref_spectra, cycle_count):
    half_width = 2 * cycle_count
    swapped = jnp.concatenate([-ref_spectra[:, :, half_width:], ref_spectra[:, :, :half_width]], axis=2)
    return jnp.concatenate([ref_spectra, swapped], axis=1)


def best_scores(part_spectra, ref_pairs, inverse):
    angles = part_spectra.shape[0]
    count_rows = part_spectra.shape[1]
    classes = ref_pairs.shape[1] // 2
    cross_terms = jnp.einsum('mnc,mkc->mnk', part_spectra.astype(jnp.float32), ref_pairs.astype(jnp.float32),
                             precision=lax.Precision.HIGHEST).astype(jnp.bfloat16)
    stacked = jnp.concatenate([cross_terms[:, :, :classes].reshape(angles, count_rows * classes),
                               cross_terms[:, :, classes:].reshape(angles, count_rows * classes)], axis=0)
    correlation = jnp.dot(inverse, stacked, preferred_element_type=jnp.float32)
    return jnp.max(correlation.reshape(angles, count_rows, classes), axis=(0, 2))


def rotate_back(weighted, rotation_rows, cycle_count):
    angles = weighted.shape[1] // (2 * cycle_count)
    shaped = weighted.reshape(weighted.shape[0], angles, 2 * cycle_count)
    doubled = jnp.concatenate([shaped, shaped], axis=1)

    def one_row(row_block, start):
        return lax.dynamic_slice_in_dim(row_block, start.astype(jnp.int32), angles, 0)

    turned = jax.vmap(one_row)(doubled, rotation_rows.astype(jnp.int32))
    return turned.reshape(weighted.shape)


def weight_columns(weights, angles):
    return jnp.tile(jnp.concatenate([weights, weights], axis=1), (1, angles))


def reference(particles, references, owner, class_offset, rotation, shifts, ctf_group, ctf_table):
    forward, inverse = angle_tables(A)
    ref_pairs = paired(spectra_of(references, forward, R), R)
    class_index = owner[:, 0] * CPD + class_offset
    blocks = P_ALL // P_DEV

    def block_step(totals, pieces):
        sums_now, weights_now = totals
        rows_in, shift_in, group_in, rotation_in, class_in = pieces
        weighted, ctf_rows = prepare(rows_in, shift_in, group_in, ctf_table)
        scores = best_scores(spectra_of(weighted, forward, R), ref_pairs, inverse)
        contrib = rotate_back(weighted, rotation_in, R)
        selector = class_in[:, None] == jnp.arange(CLASSES, dtype=jnp.int32)[None, :]
        sums_now = sums_now + jnp.dot(selector.astype(jnp.bfloat16).T, contrib, preferred_element_type=jnp.float32)
        weights_now = weights_now + jnp.dot(selector.astype(jnp.float32).T, ctf_rows * ctf_rows,
                                            precision=lax.Precision.HIGHEST, preferred_element_type=jnp.float32)
        return (sums_now, weights_now), scores

    sequence = (particles.reshape(blocks, P_DEV, 2 * A * R), shifts.reshape(blocks, P_DEV, 2),
                ctf_group.reshape(blocks, P_DEV), rotation.reshape(blocks, P_DEV), class_index.reshape(blocks, P_DEV))
    start_values = (jnp.zeros((CLASSES, 2 * A * R), jnp.float32), jnp.zeros((CLASSES, R), jnp.float32))
    (class_sums, weights), scores = lax.scan(block_step, start_values, sequence)
    new_references = class_sums / (weight_columns(weights, A) + tau_reg)
    return scores.reshape(P_ALL), new_references
```

```python
import math

import jax
import jax.numpy as jnp
from jax import lax
from jax.experimental import pallas as pl
from jax.experimental.pallas import tpu as pltpu
from jax.sharding import PartitionSpec as P

BOX = 128
SPAN = 16
EARLY = -0.5
tau_reg = 1.0
ROWS = 16
F32 = jnp.float32
BF16 = jnp.bfloat16
MESH = pl.DeviceIdType.MESH


def split_angles(angles):
    even = angles & -angles
    return even, angles // even


def lin(terms):
    total = None
    for factor, value in terms:
        if value is None or abs(factor) < 1e-12:
            continue
        if total is None:
            total = value if abs(factor - 1) < 1e-12 else (-value if abs(factor + 1) < 1e-12 else value * factor)
        elif abs(factor - 1) < 1e-12:
            total = total + value
        elif abs(factor + 1) < 1e-12:
            total = total - value
        else:
            total = total + value * factor
    return total


def add(a, b):
    return b if a is None else (a if b is None else a + b)


def sub(a, b):
    if b is None:
        return a
    return -b if a is None else a - b


def turn(re, im, part, whole):
    if part == 0:
        return re, im
    c, s = math.cos(2 * math.pi * part / whole), math.sin(2 * math.pi * part / whole)
    return lin([(c, re), (-s, im)]), lin([(s, re), (c, im)])


def three(a, b, c, sign):
    tr, ti = add(b[0], c[0]), add(b[1], c[1])
    er, ei = lin([(sign * math.sqrt(0.75), sub(b[0], c[0]))]), None
    if b[1] is not None or c[1] is not None:
        ei = lin([(sign * math.sqrt(0.75), sub(b[1], c[1]))])
    mr = sub(a[0], lin([(0.5, tr)]))
    mi = None if ti is None and a[1] is None else sub(a[1], lin([(0.5, ti)]))
    first = (add(a[0], tr), None if a[1] is None and ti is None else add(a[1], ti))
    second = (mr if ei is None else mr - ei, add(mi, er))
    third = (mr if ei is None else mr + ei, -er if mi is None else mi - er)
    return first, second, third


def nine_dft(values, sign, wanted):
    inner = [three(values[j], values[j + 3], values[j + 6], sign) for j in range(3)]
    out = {}
    for k in range(3):
        row = [turn(*inner[j][k], sign * j * k, 9) for j in range(3)]
        for l, x in enumerate(three(*row, sign)):
            out[k + 3 * l] = x
    return {k: out[k] for k in out if k in wanted}


def odd_dft(values, sign, wanted):
    n = len(values)
    if n == 9:
        return nine_dft(values, sign, wanted)
    half = n // 2
    sums = [(add(values[j][0], values[n - j][0]), add(values[j][1], values[n - j][1])) for j in range(1, half + 1)]
    diffs = [(sub(values[j][0], values[n - j][0]), sub(values[j][1], values[n - j][1])) for j in range(1, half + 1)]
    out = {}
    for k in range(half + 1):
        pair = [x for x in (k, n - k) if x in wanted]
        if not pair:
            continue
        cs = [math.cos(2 * math.pi * ((j * k) % n) / n) for j in range(1, half + 1)]
        sn = [sign * math.sin(2 * math.pi * ((j * k) % n) / n) for j in range(1, half + 1)]
        even_re = lin([(1.0, values[0][0])] + [(c, s[0]) for c, s in zip(cs, sums)])
        even_im = lin([(1.0, values[0][1])] + [(c, s[1]) for c, s in zip(cs, sums)])
        odd_re = lin([(-s, d[1]) for s, d in zip(sn, diffs)])
        odd_im = lin([(s, d[0]) for s, d in zip(sn, diffs)])
        for x in pair:
            if x == k:
                out[x] = (add(even_re, odd_re), add(even_im, odd_im))
            else:
                out[x] = (sub(even_re, odd_re), sub(even_im, odd_im))
    return out


def real_eight_dft(v):
    r = math.sqrt(0.5)
    s = [v[j] + v[j + 4] for j in range(4)]
    d = [v[j] - v[j + 4] for j in range(4)]
    a, b = s[0] + s[2], s[1] + s[3]
    p, q = r * (d[1] - d[3]), r * (d[1] + d[3])
    return [(a + b, None), (d[0] + p, -d[2] - q), (s[0] - s[2], s[3] - s[1]), (d[0] - p, d[2] - q), (a - b, None)]


def real_even_dft(values):
    n = len(values)
    if n == 8:
        return real_eight_dft(values)
    half = n // 2
    sums = [add(values[j], values[n - j]) for j in range(1, half)]
    diffs = [sub(values[j], values[n - j]) for j in range(1, half)]
    plus, minus = values[0] + values[half], values[0] - values[half]
    out = []
    for k in range(half + 1):
        cs = [math.cos(2 * math.pi * j * k / n) for j in range(1, half)]
        sn = [math.sin(2 * math.pi * j * k / n) for j in range(1, half)]
        re = lin([(1.0, minus if k % 2 else plus)] + list(zip(cs, sums)))
        im = lin([(-s, d) for s, d in zip(sn, diffs)]) if 0 < k < half else None
        out.append((re, im))
    return out


def forward_fft(load, store, angles):
    n1, n2 = split_angles(angles)
    inner = [real_even_dft([load(n2 * i + j) for i in range(n1)]) for j in range(n2)]
    for k1 in range(n1 // 2 + 1):
        values = [turn(*inner[j][k1], -((j * k1) % angles), angles) for j in range(n2)]
        for k2 in range(n2):
            pass
        wanted = set(range(n2)) if 0 < k1 < n1 // 2 else set(range(n2 // 2 + 1))
        for k2, (re, im) in odd_dft(values, -1.0, wanted).items():
            m = k1 + n1 * k2
            if m > angles // 2:
                m, im = angles - m, (None if im is None else -im)
            store(m, re, im)


def inverse_max(load, angles):
    n1, n2 = split_angles(angles)

    def value(m):
        if m == 0 or m == angles // 2:
            return load(m, 0), None
        if m > angles // 2:
            re, im = load(angles - m, 0), load(angles - m, 1)
            return re, -im
        return load(m, 0), load(m, 1)

    grid = []
    for k1 in range(n1 // 2 + 1):
        values = [value((k1 + n1 * k2) % angles) for k2 in range(n2)]
        got = odd_dft(values, 1.0, set(range(n2)))
        row = []
        for j in range(n2):
            row.append(turn(*got[j], (j * k1) % angles, angles))
        grid.append(row)
    best = None
    half = n1 // 2
    for j in range(n2):
        h0, h4 = grid[0][j][0], grid[half][j][0]
        if n1 == 8:
            r = math.sqrt(2.0)
            (a1, b1), (a2, b2), (a3, b3) = grid[1][j], grid[2][j], grid[3][j]
            plus, minus = h0 + h4, h0 - h4
            twice, sine = 2.0 * a2, 2.0 * b2
            w, e = r * (a1 - a3), r * (b1 + b3)
            tops = [plus + twice + 2.0 * jnp.abs(a1 + a3), plus - twice + 2.0 * jnp.abs(b1 - b3),
                    minus + w + jnp.abs(e + sine), minus - w + jnp.abs(e - sine)]
            for top in tops:
                best = top if best is None else jnp.maximum(best, top)
            continue
        plus, minus = h0 + h4, h0 - h4
        doubled = [(2.0 * grid[k][j][0], 2.0 * grid[k][j][1]) for k in range(1, half)]
        for i in range(half + 1):
            even = lin([(1.0, minus if i % 2 else plus)] + [(math.cos(2 * math.pi * i * (k + 1) / n1), doubled[k][0]) for k in range(half - 1)])
            odd = lin([(-math.sin(2 * math.pi * i * (k + 1) / n1), doubled[k][1]) for k in range(half - 1)]) if 0 < i < half else None
            top = even if odd is None else even + jnp.abs(odd)
            best = top if best is None else jnp.maximum(best, top)
    return best


def sin_cos_turns(u):
    u = u - jnp.floor(u + 0.5)
    v = (u * u) * (4 * math.pi * math.pi)
    s = jnp.full_like(v, 1.0 / math.factorial(17))
    for k in (15, 13, 11, 9, 7, 5, 3, 1):
        s = s * v + ((-1.0) ** (k // 2)) / math.factorial(k)
    c = jnp.full_like(v, -1.0 / math.factorial(18))
    for k in (16, 14, 12, 10, 8, 6, 4, 2, 0):
        c = c * v + ((-1.0) ** (k // 2)) / math.factorial(k)
    return s * (u * (2 * math.pi)), c


def fused(dims, part_hbm, refs_ref, shift_ref, turn_ref, owner_ref, offset_ref, group_ref, table_ref,
          best_ref, new_ref,
          part_ref, tab, phase, ctf_ref, rot_ref, meta_ref, buf, wch, ych, spec_p, spec_r, cross, contrib, got, metas, part, wpart, sbuf, rbuf, wrecv, sel_ref, keep, bsend, brecv, mid, mgot, jsend, jrecv,
          part_sem, own_sem, zsend, zrecv, psend, precv, csend, crecv, asend, arecv, msend, mrecv,
          ssend, srecv, wsend, wrecv_sem, xsend, xrecv):
    D, Z, angles, cyc = dims
    dom, zed = lax.axis_index("dom"), lax.axis_index("cls")
    rows, lanes = part_ref.shape[0], 2 * cyc
    local, width = refs_ref.shape
    pad = part.shape[1]
    bits = [1 << i for i in range(1, D.bit_length() - 1)]
    offsets = list(range(0, D, 2))
    paired = len(bits) == 2
    parity = lax.rem(dom, 2)
    last, first = 2 + 2 * parity, 4 - 2 * parity
    along = [0, D - 2] if paired else [0]

    def to_dom(q):
        return {"dom": dom ^ q, "cls": zed}

    def to_cls(j):
        return {"dom": dom, "cls": lax.rem(zed + j, Z)}

    near_first = [sorted(range(Z), key=lambda o: (abs(o - z), o)) for z in range(Z)]
    origin = [sum(jnp.where(zed == z, near_first[z][k], 0) for z in range(Z)) for k in range(Z)]

    def remote(src, dst, s, r, where):
        return pltpu.make_async_remote_copy(src_ref=src, dst_ref=dst, send_sem=s, recv_sem=r,
                                            device_id=where, device_id_type=MESH)

    def block(q, o):
        return buf.at[dom ^ q, o]

    def z_copy(src, q, o, up):
        to = {"dom": dom, "cls": zed + 1 if up else zed - 1}
        line = along.index(q)
        return remote(src, buf.at[dom ^ q, o], zsend.at[1 if up else 0, line, o], zrecv.at[line, o], to)

    def z_pass(src, q, o, moving_up, moving_down):
        @pl.when(jnp.logical_and(moving_up, zed + 1 < Z))
        def _():
            z_copy(src, q, o, True).start()

        @pl.when(jnp.logical_and(moving_down, zed > 0))
        def _():
            z_copy(src, q, o, False).start()

    def source(q, o, h):
        return refs_ref if q == 0 and h == 0 else block(q, o)

    def plane_copy(child, bit, o, h):
        q = child ^ bit
        return remote(source(q, o, h), block(q, o), psend.at[child // 2, o], precv.at[child // 2, o], to_dom(bit))

    def core_copy(q, o, h):
        return remote(source(q, o, h), block(q, o), csend.at[q // 2, o], crecv.at[q // 2, o], to_dom(1))

    def last_bit(q, h):
        return (1 << (q.bit_length() - 1)) if h % 2 == 0 else (q & -q)

    def at_hops(h, act):
        if h == 0:
            act(zed, 0)
            return
        for side in (1, -1):
            o = zed + side * h

            @pl.when(jnp.logical_and(o >= 0, o < Z))
            def _():
                act(o, side)

    fetch = pltpu.make_async_copy(part_hbm, part_ref, part_sem)
    fetch.start()
    barrier = pltpu.get_barrier_semaphore()
    for q in range(1, D):
        pl.semaphore_signal(barrier, inc=1, device_id=to_dom(q), device_id_type=MESH)
    for j in range(1, Z):
        pl.semaphore_signal(barrier, inc=1, device_id=to_cls(j), device_id_type=MESH)
    meta_ref[...] = jnp.zeros_like(meta_ref)
    meta_ref[pl.ds(0, 1), :] = owner_ref[...] * pad + offset_ref[...]
    meta_ref[pl.ds(1, 1), :] = group_ref[...]
    def column(row):
        return jnp.transpose(jnp.broadcast_to(row.astype(F32), (lanes, rows)))

    quarter, levels = angles // 4, tab.shape[1] // SPAN
    left = lax.broadcasted_iota(jnp.int32, (SPAN, lanes), 1) < cyc
    radius = (lax.rem(lax.broadcasted_iota(jnp.int32, (SPAN, lanes), 1), cyc) + 1).astype(F32) / BOX
    radius = radius * (lax.broadcasted_iota(jnp.int32, (SPAN, lanes), 0) - SPAN // 2).astype(F32)
    for a in range(quarter + 1):
        s, c = sin_cos_turns(radius * (math.cos(2 * math.pi * a / angles) if a < quarter else 0.0))
        for h, value in enumerate((c, jnp.where(left, -s, s))):
            for n in range(levels):
                tab[a, pl.ds(n * SPAN, SPAN), pl.ds(h * lanes, lanes)] = value.astype(BF16)
                value = value - value.astype(BF16).astype(F32)
    moved = jnp.concatenate([column(shift_ref[pl.ds(n, 1), :]) for n in range(2)], axis=0).astype(jnp.int32)
    steps = lax.rem(lax.broadcasted_iota(jnp.int32, (2 * rows, levels * SPAN), 1), SPAN) - SPAN // 2
    picked = jnp.where(moved[:, :levels * SPAN] == steps, 1.0, 0.0).astype(BF16)
    for a in range(quarter + 1):
        phase[a] = jnp.dot(picked, tab[a], preferred_element_type=F32)
    rot_ref[...] = column(turn_ref[...]).astype(jnp.int32)
    groups = table_ref.shape[0]
    table = table_ref[...]
    gcol = column(group_ref[...]).astype(jnp.int32)
    gcol = jnp.concatenate([gcol] * -(-groups // lanes), axis=1)[:, :groups]
    pick = jnp.where(gcol == lax.broadcasted_iota(jnp.int32, (rows, groups), 1), 1.0, 0.0)
    one = jnp.dot(pick, table, precision=lax.Precision.HIGHEST, preferred_element_type=F32)
    ctf_ref[...] = jnp.concatenate([one, one], axis=1)

    pl.semaphore_wait(barrier, D + Z - 2)

    own = pltpu.make_async_copy(refs_ref, buf.at[dom, zed], own_sem)
    own.start()
    z_pass(refs_ref, 0, zed, zed >= 0, zed >= 0)

    def children(q, h):
        return [(q ^ b, b) for b in bits if not q & b and last_bit(q ^ b, h) == b]

    def event(q, h):
        def act(o, side):
            if h and q in along:
                z_copy(refs_ref, q, o, True).wait_recv()
                if side < 0:
                    z_pass(block(q, o), q, o, zed >= 0, zed < 0)
                else:
                    z_pass(block(q, o), q, o, zed < 0, zed >= 0)
            elif q:
                plane_copy(q, last_bit(q, h), o, h).wait_recv()
                if q in along:
                    z_pass(block(q, o), q, o, zed >= 0, zed >= 0)
            if not paired or q == 0:
                for child, b in children(q, h):
                    if not paired or child not in along:
                        plane_copy(child, b, o, h).start()
            elif h == 0 and q not in along:
                @pl.when(first == D - 2 - q)
                def _():
                    plane_copy(D - 2, D - 2 - q, o, h).start()
            core_copy(q, o, h).start()

        at_hops(h, act)

    event(0, 0)
    for q in range(1, D):
        remote(meta_ref, metas.at[q], msend.at[q], mrecv.at[q], to_dom(q)).start()
    metas[0] = meta_ref[...]

    plan = {}
    for h in range(Z):
        for q in sorted(offsets, key=lambda q: bin(q).count("1")):
            hops = bin(q).count("1")
            if not q and not h:
                continue
            if not paired:
                spot = ("fft", h)
            elif hops == 0:
                spot = ("prep", 4) if h == 1 else ("prep", 7) if h == 2 else ("counted", 0) if h == 3 else ("fft", h - 1)
            elif hops == 1:
                spot = ("prep", 4) if h == 0 else ("summed", 0) if h == 1 else ("fft", h)
            else:
                spot = ("sent", 0) if h == 0 else ("fft", h)
            plan.setdefault(spot, []).append((q, h))

    def serve(*spot):
        for q, h in plan.get(spot, []):
            event(q, h)

    fetch.wait()
    chunks = rows // ROWS
    low, high = split_angles(angles)

    def piece(ref, sl, a):
        if width % lanes == 0:
            return ref(a * lanes // width)[sl, pl.ds(a * lanes % width, lanes)]
        halves = [(a * lanes + h * cyc) for h in range(2)]
        return jnp.concatenate([ref(c // width)[sl, pl.ds(c % width, cyc)] for c in halves], axis=1)

    def twin_copy(i):
        start = pl.multiple_of(i * ROWS, ROWS)
        return remote(contrib.at[1, :, pl.ds(start, ROWS), :], contrib.at[0, :, pl.ds(rows + start, ROWS), :],
                      xsend.at[i], xrecv.at[i], to_dom(1))

    def prep_chunk(i, carry):
        sl = pl.ds(pl.multiple_of(i * ROWS, ROWS), ROWS)
        ctf = ctf_ref[sl, :]
        also = pl.ds(pl.multiple_of(rows + i * ROWS, ROWS), ROWS)

        def apply(a, c, s):
            for b, sign in ((a, 1), (a + angles // 2, -1)):
                x = part_ref[sl, pl.ds(b * lanes, lanes)].astype(F32)
                y = pltpu.roll(x, cyc, 1) * s
                wch[b] = (x * c + y if sign > 0 else x * c - y).astype(BF16)

        for a in range(quarter + 1):
            cx, sx = phase[a, sl, pl.ds(0, lanes)], phase[a, sl, pl.ds(lanes, lanes)]
            cy = phase[quarter - a, also, pl.ds(0, lanes)] * ctf
            sy = phase[quarter - a, also, pl.ds(lanes, lanes)] * ctf
            cc, ss, sc, cs = cx * cy, sx * sy, sx * cy, cx * sy
            apply(a, cc - ss, sc + cs)
            if 0 < a < quarter:
                apply(angles // 2 - a, cc + ss, cs - sc)

        def store(m, re, im):
            first = re.astype(BF16)
            second = jnp.zeros_like(first) if im is None else im.astype(BF16)
            lower = pl.ds(pl.multiple_of(rows + i * ROWS, ROWS), ROWS)
            spec_p[m, sl, pl.ds(0, lanes)] = first
            spec_p[m, sl, pl.ds(lanes, lanes)] = second
            spec_p[m, lower, pl.ds(0, lanes)] = second
            spec_p[m, lower, pl.ds(lanes, lanes)] = -first

        forward_fft(lambda a: wch[a].astype(F32), store, angles)
        rot = rot_ref[sl, :]
        bits_on = [jnp.where((rot & (1 << n)) != 0, 1.0, 0.0).astype(BF16) > 0 for n in range((angles - 1).bit_length())]
        memo = {}

        def staged(level, a):
            a = a % angles
            if (level, a) not in memo:
                if level == 0:
                    memo[level, a] = wch[a]
                else:
                    step = 1 << (level - 1)
                    on = bits_on[level - 1]
                    memo[level, a] = jnp.where(on, staged(level - 1, a + step), staged(level - 1, a))
            return memo[level, a]

        levels = low.bit_length() - 1
        for a in range(angles):
            ych[a] = staged(levels, a)
        for r in range(low):
            line = [ych[r + low * j] for j in range(high)]
            for bit in range((high - 1).bit_length()):
                on = bits_on[levels + bit]
                line = [jnp.where(on, line[(j + (1 << bit)) % high], line[j]) for j in range(high)]
            for j in range(high):
                a = r + low * j
                value = line[j]
                if paired:
                    d = a * lanes // width
                    contrib[parity if d % 2 == 0 else 1 - parity, d // 2, sl, pl.ds(a * lanes % width, lanes)] = value
                elif width % lanes == 0:
                    contrib[a * lanes // width, sl, pl.ds(a * lanes % width, lanes)] = value
                else:
                    for h in range(2):
                        col = a * lanes + h * cyc
                        contrib[col // width, sl, pl.ds(col % width, cyc)] = value[:, h * cyc:(h + 1) * cyc]
        if paired:
            @pl.when(i > 0)
            def _():
                twin_copy(i - 1).start()
        for c in range(chunks):
            if ("prep", c) in plan:
                @pl.when(i == c)
                def _():
                    serve("prep", c)
        return carry

    lax.fori_loop(0, chunks, prep_chunk, 0)

    spans = [(0, width)]
    if width % lanes == 0 and width // lanes >= 3:
        n = width // lanes
        cuts = [0, n - n // 3 - max(1, n * 2 // 9), n - max(1, n * 2 // 9), n]
        spans = [(x * lanes, (y - x) * lanes) for x, y in zip(cuts[:-1], cuts[1:])]

    def contrib_copy(q, c):
        cols = pl.ds(*spans[c])
        return remote(contrib.at[dom ^ q, :, cols], got.at[q, :, cols], asend.at[q, c], arecv.at[q, c], to_dom(q))

    def half_copy(h, c):
        cols = pl.ds(*spans[c])
        return remote(bsend.at[h, :, :, cols], brecv.at[h, :, :, cols], asend.at[h, c], arecv.at[h, c],
                      {"dom": dom ^ first, "cls": zed})

    def joined(c):
        cols = pl.ds(*spans[c])
        return remote(mid.at[:, :, cols], mgot.at[:, :, cols], jsend.at[c], jrecv.at[c], {"dom": dom ^ last, "cls": zed})

    if paired:
        twin_copy(chunks - 1).start()
    else:
        for c in range(len(spans)):
            for q in range(1, D):
                contrib_copy(q, c).start()
        got[0] = contrib[dom]

    for q in range(1, D):
        remote(meta_ref, metas.at[q], msend.at[q], mrecv.at[q], to_dom(q)).wait()
    ids = lax.broadcasted_iota(jnp.int32, (Z * pad, rows), 0)
    gids = lax.broadcasted_iota(jnp.int32, (groups, rows), 0)
    sel_ref[...] = jnp.concatenate([jnp.where(ids == metas[d, pl.ds(0, 1), :], 1.0, 0.0).astype(BF16) for d in range(D)], axis=1)
    if paired:
        for i in range(chunks):
            twin_copy(i).wait_recv()
        for h, chip in enumerate((dom ^ first ^ last, dom ^ first, dom ^ last, dom)):
            for c, (start, size) in enumerate(spans):
                cols = pl.ds(start, size)
                sums = jnp.dot(sel_ref[:, pl.ds(0, 2 * rows)], contrib[0, chip // 2, :, cols], preferred_element_type=F32)
                sums = sums.reshape(Z, pad, size)[:, :local, :]
                if h == 1 and c == 0:
                    serve("sent", 0)
                if h < 2:
                    bsend[h, :, :, cols] = sums.astype(BF16)
                    half_copy(h, c).start()
                elif h == 2:
                    keep[:, pl.ds(0, local), cols] = sums
                else:
                    part[:, pl.ds(0, local), cols] = sums
        serve("summed", 0)
    gsel = jnp.concatenate([jnp.where(gids == metas[d, pl.ds(1, 1), :], 1.0, 0.0).astype(BF16) for d in range(D)], axis=1)
    counts = lax.dot_general(sel_ref[...], gsel, (((1,), (1,)), ((), ())), preferred_element_type=F32)
    wsum = jnp.dot(counts, table * table, precision=lax.Precision.HIGHEST, preferred_element_type=F32)
    wpart[...] = wsum.reshape(Z, pad, wsum.shape[1])

    def w_copy(j):
        return remote(wpart.at[lax.rem(zed + j, Z)], wrecv.at[j], wsend.at[j], wrecv_sem.at[j], to_cls(j))

    for j in range(1, Z):
        w_copy(j).start()

    def s_copy(j, c):
        cols = pl.ds(*spans[c])
        return remote(sbuf.at[lax.rem(zed + j, Z), :, cols], rbuf.at[j, :, cols], ssend.at[j, c], srecv.at[j, c], to_cls(j))

    def send_span(c):
        start, size = spans[c]
        cols = pl.ds(start, size)
        if paired:
            half_copy(1, c).wait_recv()
            joined(c).wait_recv()
            both = brecv[1, :, :, cols].astype(F32) + mgot[:, :, cols].astype(F32)
            part[:, pl.ds(0, local), cols] = part[:, pl.ds(0, local), cols] + both
        else:
            for q in range(1, D):
                contrib_copy(q, c).wait()
            sums = jnp.dot(sel_ref[...], got[:, :, cols].reshape(D * rows, size), preferred_element_type=F32)
            part[:, :, cols] = sums.reshape(Z, pad, size)
        sbuf[:, :, cols] = part[:, pl.ds(0, local), cols].astype(BF16)
        for j in range(1, Z):
            s_copy(j, c).start()

    serve("counted", 0)
    own.wait()

    def ref_rows(z, start, count):
        sl = pl.ds(start, count)
        out = pl.ds(start, count)

        def store(m, re, im):
            second = jnp.zeros_like(re) if im is None else im
            spec_r[m, z, out, pl.ds(0, lanes)] = re.astype(BF16)
            spec_r[m, z, out, pl.ds(lanes, lanes)] = second.astype(BF16)

        forward_fft(lambda a: piece(lambda d: buf.at[d, z], sl, a).astype(F32), store, angles)

    whole = local // ROWS
    rest = local % ROWS

    def pass_on():
        for c, (start, size) in enumerate(spans):
            cols = pl.ds(start, size)
            half_copy(0, c).wait_recv()
            mid[:, :, cols] = (keep[:, pl.ds(0, local), cols] + brecv[0, :, :, cols].astype(F32)).astype(BF16)
            joined(c).start()

    def ref_step(n, carry):
        k = n // whole
        for c in range(Z):
            @pl.when(n == c * whole)
            def _():
                if paired and c == Z - 1:
                    pass_on()
                serve("fft", c)
                for q in offsets:
                    core_copy(q, origin[c], 1).wait_recv()

        z = sum(jnp.where(k == c, origin[c], 0) for c in range(Z))
        ref_rows(z, pl.multiple_of((n % whole) * ROWS, ROWS), ROWS)
        return carry

    lax.fori_loop(0, Z * whole, ref_step, 0)
    if rest:
        def ref_rest(z, carry):
            ref_rows(z, whole * ROWS, rest)
            return carry
        lax.fori_loop(0, Z, ref_rest, 0)

    freqs = angles // 2 + 1

    def cross_step(m, carry):
        lhs = spec_r[m].reshape(Z * pad, 2 * lanes)
        cross[m] = lax.dot_general(lhs, spec_p[m], (((1,), (1,)), ((), ())), preferred_element_type=F32)
        return carry

    group = 4

    def cross_group(n, carry):
        for g in range(group):
            cross_step(n * group + g, carry)
        return carry

    groups_of = -(-local // 8)

    def back_step(n, best):
        z, j = n // groups_of, n % groups_of
        start = pl.multiple_of(z * pad + j * 8, 8)

        def load(m, p):
            return cross[m, pl.ds(start, 8), pl.ds(p * rows, rows)]

        top = inverse_max(load, angles)
        row = lax.broadcasted_iota(jnp.int32, (8, rows), 0) + j * 8
        return jnp.maximum(best, jnp.where(row < local, top, -jnp.inf))

    pieces = freqs // group
    half_way, in_all = (pieces + 1) // 2, Z * groups_of
    lax.fori_loop(0, half_way, cross_group, 0)
    send_span(0)
    lax.fori_loop(half_way, pieces, cross_group, 0)
    for m in range(pieces * group, freqs):
        cross_step(m, 0)
    for c in range(1, len(spans) - 1):
        send_span(c)
    best = lax.fori_loop(0, in_all // 2, back_step, jnp.full((8, rows), -jnp.inf, F32))
    for c in range(max(1, len(spans) - 1), len(spans)):
        send_span(c)
    best = lax.fori_loop(in_all // 2, in_all, back_step, best)
    best_ref[...] = jnp.max(best, axis=0, keepdims=True) * (1.0 / angles)

    weight = wpart[zed][:local, :]
    for j in range(1, Z):
        w_copy(j).wait()
        weight = weight + wrecv[j][:local, :]
    scale = 1.0 / (jnp.concatenate([weight, weight], axis=1) + tau_reg)
    for c, (start, size) in enumerate(spans):
        cols = pl.ds(start, size)
        total = part[zed, :, cols][:local, :]
        for j in range(1, Z):
            s_copy(j, c).wait()
            total = total + rbuf[j, :, cols].astype(F32)
        new_ref[:, cols] = total * jnp.concatenate([scale] * -(-size // lanes), axis=1)[:, :size]

    if paired:
        for c in range(len(spans)):
            joined(c).wait_send()
            for h in range(2):
                half_copy(h, c).wait_send()
        for i in range(chunks):
            twin_copy(i).wait_send()
    for q in along:
        for o in range(Z):
            @pl.when(jnp.logical_and(o <= zed, zed + 1 < Z))
            def _():
                z_copy(refs_ref, q, o, True).wait_send()

            @pl.when(jnp.logical_and(o >= zed, zed > 0))
            def _():
                z_copy(refs_ref, q, o, False).wait_send()
    for o in range(Z):
        for q in offsets:
            core_copy(q, o, 1).wait_send()
            if q and q not in along:
                plane_copy(q, last_bit(q, 1), o, 1).wait_send()
    if paired:
        plane_copy(D - 2, 2, zed, 0).wait_send()


def per_device(particles, references, owner, class_offset, rotation, shifts, ctf_group, ctf_table):
    D, Z = lax.axis_size("dom"), lax.axis_size("cls")
    groups, cyc = ctf_table.shape
    rows, full = particles.shape
    lanes = 2 * cyc
    angles = full // lanes
    local, width = references.shape
    pad = -(-local // ROWS) * ROWS
    freqs = angles // 2 + 1
    chunks = 3
    dma = pltpu.SemaphoreType.DMA
    paired = D == 8
    best, new = pl.pallas_call(
        lambda *refs: fused((D, Z, angles, cyc), *refs),
        out_shape=(jax.ShapeDtypeStruct((1, rows), F32), jax.ShapeDtypeStruct((local, width), F32)),
        in_specs=[pl.BlockSpec(memory_space=pl.ANY)] * 2 + [pl.BlockSpec(memory_space=pltpu.VMEM)] * 6,
        out_specs=[pl.BlockSpec(memory_space=pltpu.VMEM)] * 2,
        scratch_shapes=[
            pltpu.VMEM((rows, full), BF16),
            pltpu.VMEM((angles // 4 + 1, 3 * SPAN, 2 * lanes), BF16),
            pltpu.VMEM((angles // 4 + 1, 2 * rows, 2 * lanes), F32),
            pltpu.VMEM((rows, lanes), F32),
            pltpu.VMEM((rows, lanes), jnp.int32),
            pltpu.VMEM((8, rows), jnp.int32),
            pltpu.VMEM((D, Z, local, width), BF16),
            pltpu.VMEM((angles, ROWS, lanes), BF16),
            pltpu.VMEM((angles, ROWS, lanes), BF16),
            pltpu.VMEM((freqs, 2 * rows, 2 * lanes), BF16),
            pltpu.VMEM((freqs, Z, pad, 2 * lanes), BF16),
            pltpu.VMEM((freqs, Z * pad, 2 * rows), F32),
            pltpu.VMEM((2, D // 2, 2 * rows, width) if paired else (D, rows, width), BF16),
            pltpu.VMEM((1, ROWS, lanes) if paired else (D, rows, width), BF16),
            pltpu.VMEM((D, 8, rows), jnp.int32),
            pltpu.VMEM((Z, pad, width), F32),
            pltpu.VMEM((Z, pad, cyc), F32),
            pltpu.VMEM((Z, local, width), BF16),
            pltpu.VMEM((Z, local, width), BF16),
            pltpu.VMEM((Z, pad, cyc), F32),
            pltpu.VMEM((Z * pad, D * rows), BF16),
            pltpu.VMEM((Z, pad, width) if paired else (1, 8, lanes), F32),
            pltpu.VMEM((2, Z, local, width) if paired else (1, 1, ROWS, lanes), BF16),
            pltpu.VMEM((2, Z, local, width) if paired else (1, 1, ROWS, lanes), BF16),
            pltpu.VMEM((Z, local, width), BF16),
            pltpu.VMEM((Z, local, width), BF16),
            dma((chunks,)), dma((chunks,)),
            dma, dma, dma((2, 2, Z)), dma((2, Z)),
            dma((D // 2, Z)), dma((D // 2, Z)), dma((D // 2, Z)), dma((D // 2, Z)),
            dma((D, chunks)), dma((D, chunks)), dma((D,)), dma((D,)),
            dma((Z, chunks)), dma((Z, chunks)), dma((Z,)), dma((Z,)),
            dma((rows // ROWS,)), dma((rows // ROWS,)),
        ],
        compiler_params=pltpu.CompilerParams(collective_id=0, has_side_effects=True,
                                             vmem_limit_bytes=60 << 20),
        name="class_pass",
    )(particles, references, shifts.T, rotation[None], owner.T, class_offset[None], ctf_group[None], ctf_table)
    return best[0], new


def solution(mesh):
    return jax.shard_map(
        per_device,
        mesh=mesh,
        in_specs=(
            P(("dom", "cls"), None),
            P("cls", "dom"),
            P(("dom", "cls"), None),
            P(("dom", "cls")),
            P(("dom", "cls")),
            P(("dom", "cls"), None),
            P(("dom", "cls")),
            P(),
        ),
        out_specs=(P(("dom", "cls")), P("cls", "dom")),
        check_vma=False,
    )
```

```python
import math

import jax
import jax.numpy as jnp
from jax import lax
from jax.experimental import pallas as pl
from jax.experimental.pallas import tpu as pltpu
from jax.sharding import PartitionSpec as P

BOX = 128
SPAN = 16
EARLY = -0.5
tau_reg = 1.0
ROWS = 16
F32 = jnp.float32
BF16 = jnp.bfloat16
MESH = pl.DeviceIdType.MESH


def split_angles(angles):
    even = angles & -angles
    return even, angles // even


def lin(terms):
    total = None
    for factor, value in terms:
        if value is None or abs(factor) < 1e-12:
            continue
        if total is None:
            total = value if abs(factor - 1) < 1e-12 else (-value if abs(factor + 1) < 1e-12 else value * factor)
        elif abs(factor - 1) < 1e-12:
            total = total + value
        elif abs(factor + 1) < 1e-12:
            total = total - value
        else:
            total = total + value * factor
    return total


def add(a, b):
    return b if a is None else (a if b is None else a + b)


def sub(a, b):
    if b is None:
        return a
    return -b if a is None else a - b


def turn(re, im, part, whole):
    if part == 0:
        return re, im
    c, s = math.cos(2 * math.pi * part / whole), math.sin(2 * math.pi * part / whole)
    return lin([(c, re), (-s, im)]), lin([(s, re), (c, im)])


def three(a, b, c, sign):
    tr, ti = add(b[0], c[0]), add(b[1], c[1])
    er, ei = lin([(sign * math.sqrt(0.75), sub(b[0], c[0]))]), None
    if b[1] is not None or c[1] is not None:
        ei = lin([(sign * math.sqrt(0.75), sub(b[1], c[1]))])
    mr = sub(a[0], lin([(0.5, tr)]))
    mi = None if ti is None and a[1] is None else sub(a[1], lin([(0.5, ti)]))
    first = (add(a[0], tr), None if a[1] is None and ti is None else add(a[1], ti))
    second = (mr if ei is None else mr - ei, add(mi, er))
    third = (mr if ei is None else mr + ei, -er if mi is None else mi - er)
    return first, second, third


def nine_dft(values, sign, wanted):
    inner = [three(values[j], values[j + 3], values[j + 6], sign) for j in range(3)]
    out = {}
    for k in range(3):
        row = [turn(*inner[j][k], sign * j * k, 9) for j in range(3)]
        for l, x in enumerate(three(*row, sign)):
            out[k + 3 * l] = x
    return {k: out[k] for k in out if k in wanted}


def odd_dft(values, sign, wanted):
    n = len(values)
    if n == 9:
        return nine_dft(values, sign, wanted)
    half = n // 2
    sums = [(add(values[j][0], values[n - j][0]), add(values[j][1], values[n - j][1])) for j in range(1, half + 1)]
    diffs = [(sub(values[j][0], values[n - j][0]), sub(values[j][1], values[n - j][1])) for j in range(1, half + 1)]
    out = {}
    for k in range(half + 1):
        pair = [x for x in (k, n - k) if x in wanted]
        if not pair:
            continue
        cs = [math.cos(2 * math.pi * ((j * k) % n) / n) for j in range(1, half + 1)]
        sn = [sign * math.sin(2 * math.pi * ((j * k) % n) / n) for j in range(1, half + 1)]
        even_re = lin([(1.0, values[0][0])] + [(c, s[0]) for c, s in zip(cs, sums)])
        even_im = lin([(1.0, values[0][1])] + [(c, s[1]) for c, s in zip(cs, sums)])
        odd_re = lin([(-s, d[1]) for s, d in zip(sn, diffs)])
        odd_im = lin([(s, d[0]) for s, d in zip(sn, diffs)])
        for x in pair:
            if x == k:
                out[x] = (add(even_re, odd_re), add(even_im, odd_im))
            else:
                out[x] = (sub(even_re, odd_re), sub(even_im, odd_im))
    return out


def real_eight_dft(v):
    r = math.sqrt(0.5)
    s = [v[j] + v[j + 4] for j in range(4)]
    d = [v[j] - v[j + 4] for j in range(4)]
    a, b = s[0] + s[2], s[1] + s[3]
    p, q = r * (d[1] - d[3]), r * (d[1] + d[3])
    return [(a + b, None), (d[0] + p, -d[2] - q), (s[0] - s[2], s[3] - s[1]), (d[0] - p, d[2] - q), (a - b, None)]


def real_even_dft(values):
    n = len(values)
    if n == 8:
        return real_eight_dft(values)
    half = n // 2
    sums = [add(values[j], values[n - j]) for j in range(1, half)]
    diffs = [sub(values[j], values[n - j]) for j in range(1, half)]
    plus, minus = values[0] + values[half], values[0] - values[half]
    out = []
    for k in range(half + 1):
        cs = [math.cos(2 * math.pi * j * k / n) for j in range(1, half)]
        sn = [math.sin(2 * math.pi * j * k / n) for j in range(1, half)]
        re = lin([(1.0, minus if k % 2 else plus)] + list(zip(cs, sums)))
        im = lin([(-s, d) for s, d in zip(sn, diffs)]) if 0 < k < half else None
        out.append((re, im))
    return out


def forward_fft(load, store, angles):
    n1, n2 = split_angles(angles)
    inner = [real_even_dft([load(n2 * i + j) for i in range(n1)]) for j in range(n2)]
    for k1 in range(n1 // 2 + 1):
        values = [turn(*inner[j][k1], -((j * k1) % angles), angles) for j in range(n2)]
        for k2 in range(n2):
            pass
        wanted = set(range(n2)) if 0 < k1 < n1 // 2 else set(range(n2 // 2 + 1))
        for k2, (re, im) in odd_dft(values, -1.0, wanted).items():
            m = k1 + n1 * k2
            if m > angles // 2:
                m, im = angles - m, (None if im is None else -im)
            store(m, re, im)


def inverse_max(load, angles):
    n1, n2 = split_angles(angles)

    def value(m):
        if m == 0 or m == angles // 2:
            return load(m, 0), None
        if m > angles // 2:
            re, im = load(angles - m, 0), load(angles - m, 1)
            return re, -im
        return load(m, 0), load(m, 1)

    grid = []
    for k1 in range(n1 // 2 + 1):
        values = [value((k1 + n1 * k2) % angles) for k2 in range(n2)]
        got = odd_dft(values, 1.0, set(range(n2)))
        row = []
        for j in range(n2):
            row.append(turn(*got[j], (j * k1) % angles, angles))
        grid.append(row)
    best = None
    half = n1 // 2
    for j in range(n2):
        h0, h4 = grid[0][j][0], grid[half][j][0]
        if n1 == 8:
            r = math.sqrt(2.0)
            (a1, b1), (a2, b2), (a3, b3) = grid[1][j], grid[2][j], grid[3][j]
            plus, minus = h0 + h4, h0 - h4
            twice, sine = 2.0 * a2, 2.0 * b2
            w, e = r * (a1 - a3), r * (b1 + b3)
            tops = [plus + twice + 2.0 * jnp.abs(a1 + a3), plus - twice + 2.0 * jnp.abs(b1 - b3),
                    minus + w + jnp.abs(e + sine), minus - w + jnp.abs(e - sine)]
            for top in tops:
                best = top if best is None else jnp.maximum(best, top)
            continue
        plus, minus = h0 + h4, h0 - h4
        doubled = [(2.0 * grid[k][j][0], 2.0 * grid[k][j][1]) for k in range(1, half)]
        for i in range(half + 1):
            even = lin([(1.0, minus if i % 2 else plus)] + [(math.cos(2 * math.pi * i * (k + 1) / n1), doubled[k][0]) for k in range(half - 1)])
            odd = lin([(-math.sin(2 * math.pi * i * (k + 1) / n1), doubled[k][1]) for k in range(half - 1)]) if 0 < i < half else None
            top = even if odd is None else even + jnp.abs(odd)
            best = top if best is None else jnp.maximum(best, top)
    return best


def sin_cos_turns(u):
    u = u - jnp.floor(u + 0.5)
    v = (u * u) * (4 * math.pi * math.pi)
    s = jnp.full_like(v, 1.0 / math.factorial(17))
    for k in (15, 13, 11, 9, 7, 5, 3, 1):
        s = s * v + ((-1.0) ** (k // 2)) / math.factorial(k)
    c = jnp.full_like(v, -1.0 / math.factorial(18))
    for k in (16, 14, 12, 10, 8, 6, 4, 2, 0):
        c = c * v + ((-1.0) ** (k // 2)) / math.factorial(k)
    return s * (u * (2 * math.pi)), c


def fused(dims, part_hbm, refs_ref, shift_ref, turn_ref, owner_ref, offset_ref, group_ref, table_ref,
          best_ref, new_ref,
          part_ref, tab, phase, ctf_ref, rot_ref, meta_ref, buf, wch, ych, spec_p, spec_r, cross, contrib, got, metas, part, wpart, sbuf, rbuf, wrecv, sel_ref, keep, bsend, brecv, mid, mgot, jsend, jrecv,
          part_sem, own_sem, zsend, zrecv, psend, precv, csend, crecv, asend, arecv, msend, mrecv,
          ssend, srecv, wsend, wrecv_sem, xsend, xrecv):
    D, Z, angles, cyc = dims
    dom, zed = lax.axis_index("dom"), lax.axis_index("cls")
    rows, lanes = part_ref.shape[0], 2 * cyc
    local, width = refs_ref.shape
    pad = part.shape[1]
    bits = [1 << i for i in range(1, D.bit_length() - 1)]
    offsets = list(range(0, D, 2))
    paired = len(bits) == 2 and Z == 4
    parity = lax.rem(dom, 2)
    last, first = 2 + 2 * parity, 4 - 2 * parity
    along = [0, D - 2] if paired else [0]

    def to_dom(q):
        return {"dom": dom ^ q, "cls": zed}

    def to_cls(j):
        return {"dom": dom, "cls": lax.rem(zed + j, Z)}

    near_first = [sorted(range(Z), key=lambda o: (abs(o - z), o)) for z in range(Z)]
    origin = [sum(jnp.where(zed == z, near_first[z][k], 0) for z in range(Z)) for k in range(Z)]

    def remote(src, dst, s, r, where):
        return pltpu.make_async_remote_copy(src_ref=src, dst_ref=dst, send_sem=s, recv_sem=r,
                                            device_id=where, device_id_type=MESH)

    def block(q, o):
        return buf.at[dom ^ q, o]

    def z_copy(src, q, o, up):
        to = {"dom": dom, "cls": zed + 1 if up else zed - 1}
        line = along.index(q)
        return remote(src, buf.at[dom ^ q, o], zsend.at[1 if up else 0, line, o], zrecv.at[line, o], to)

    def z_pass(src, q, o, moving_up, moving_down):
        @pl.when(jnp.logical_and(moving_up, zed + 1 < Z))
        def _():
            z_copy(src, q, o, True).start()

        @pl.when(jnp.logical_and(moving_down, zed > 0))
        def _():
            z_copy(src, q, o, False).start()

    def source(q, o, h):
        return refs_ref if q == 0 and h == 0 else block(q, o)

    def plane_copy(child, bit, o, h):
        q = child ^ bit
        return remote(source(q, o, h), block(q, o), psend.at[child // 2, o], precv.at[child // 2, o], to_dom(bit))

    def core_copy(q, o, h):
        return remote(source(q, o, h), block(q, o), csend.at[q // 2, o], crecv.at[q // 2, o], to_dom(1))

    def last_bit(q, h):
        return (1 << (q.bit_length() - 1)) if h % 2 == 0 else (q & -q)

    def at_hops(h, act):
        if h == 0:
            act(zed, 0)
            return
        for side in (1, -1):
            o = zed + side * h

            @pl.when(jnp.logical_and(o >= 0, o < Z))
            def _():
                act(o, side)

    fetch = pltpu.make_async_copy(part_hbm, part_ref, part_sem)
    fetch.start()
    barrier = pltpu.get_barrier_semaphore()
    for q in range(1, D):
        pl.semaphore_signal(barrier, inc=1, device_id=to_dom(q), device_id_type=MESH)
    for j in range(1, Z):
        pl.semaphore_signal(barrier, inc=1, device_id=to_cls(j), device_id_type=MESH)
    meta_ref[...] = jnp.zeros_like(meta_ref)
    meta_ref[pl.ds(0, 1), :] = owner_ref[...] * pad + offset_ref[...]
    meta_ref[pl.ds(1, 1), :] = group_ref[...]
    def column(row):
        return jnp.transpose(jnp.broadcast_to(row.astype(F32), (lanes, rows)))

    quarter, levels = angles // 4, tab.shape[1] // SPAN
    left = lax.broadcasted_iota(jnp.int32, (SPAN, lanes), 1) < cyc
    radius = (lax.rem(lax.broadcasted_iota(jnp.int32, (SPAN, lanes), 1), cyc) + 1).astype(F32) / BOX
    radius = radius * (lax.broadcasted_iota(jnp.int32, (SPAN, lanes), 0) - SPAN // 2).astype(F32)
    for a in range(quarter + 1):
        s, c = sin_cos_turns(radius * (math.cos(2 * math.pi * a / angles) if a < quarter else 0.0))
        for h, value in enumerate((c, jnp.where(left, -s, s))):
            for n in range(levels):
                tab[a, pl.ds(n * SPAN, SPAN), pl.ds(h * lanes, lanes)] = value.astype(BF16)
                value = value - value.astype(BF16).astype(F32)
    moved = jnp.concatenate([column(shift_ref[pl.ds(n, 1), :]) for n in range(2)], axis=0).astype(jnp.int32)
    steps = lax.rem(lax.broadcasted_iota(jnp.int32, (2 * rows, levels * SPAN), 1), SPAN) - SPAN // 2
    picked = jnp.where(moved[:, :levels * SPAN] == steps, 1.0, 0.0).astype(BF16)
    for a in range(quarter + 1):
        phase[a] = jnp.dot(picked, tab[a], preferred_element_type=F32)
    rot_ref[...] = column(turn_ref[...]).astype(jnp.int32)
    groups = table_ref.shape[0]
    table = table_ref[...]
    gcol = column(group_ref[...]).astype(jnp.int32)
    gcol = jnp.concatenate([gcol] * -(-groups // lanes), axis=1)[:, :groups]
    pick = jnp.where(gcol == lax.broadcasted_iota(jnp.int32, (rows, groups), 1), 1.0, 0.0)
    one = jnp.dot(pick, table, precision=lax.Precision.HIGHEST, preferred_element_type=F32)
    ctf_ref[...] = jnp.concatenate([one, one], axis=1)

    pl.semaphore_wait(barrier, D + Z - 2)

    own = pltpu.make_async_copy(refs_ref, buf.at[dom, zed], own_sem)
    own.start()
    z_pass(refs_ref, 0, zed, zed >= 0, zed >= 0)

    def children(q, h):
        return [(q ^ b, b) for b in bits if not q & b and last_bit(q ^ b, h) == b]

    def event(q, h, only=None):
        def act(o, side):
            if only == "plane":
                pass
            elif h and q in along:
                z_copy(refs_ref, q, o, True).wait_recv()
                if side < 0:
                    z_pass(block(q, o), q, o, zed >= 0, zed < 0)
                else:
                    z_pass(block(q, o), q, o, zed < 0, zed >= 0)
            elif q:
                plane_copy(q, last_bit(q, h), o, h).wait_recv()
                if q in along:
                    z_pass(block(q, o), q, o, zed >= 0, zed >= 0)
            if only == "line":
                return
            if not paired or q == 0:
                for child, b in children(q, h):
                    if not paired or child not in along:
                        plane_copy(child, b, o, h).start()
            elif h == 0 and q not in along:
                @pl.when(first == D - 2 - q)
                def _():
                    plane_copy(D - 2, D - 2 - q, o, h).start()
            core_copy(q, o, h).start()

        at_hops(h, act)

    event(0, 0)
    for q in range(1, D):
        remote(meta_ref, metas.at[q], msend.at[q], mrecv.at[q], to_dom(q)).start()
    metas[0] = meta_ref[...]

    plan = {("prep", 4): [(0, 1, "line")], ("prep", 5): [(2, 0), (4, 0), (0, 1, "plane")]} if paired else {}

    def serve(*pairs):
        for q, h, *part_of in pairs:
            if h < Z:
                event(q, h, *part_of)

    fetch.wait()
    chunks = rows // ROWS
    low, high = split_angles(angles)

    def piece(ref, sl, a):
        if width % lanes == 0:
            return ref(a * lanes // width)[sl, pl.ds(a * lanes % width, lanes)]
        halves = [(a * lanes + h * cyc) for h in range(2)]
        return jnp.concatenate([ref(c // width)[sl, pl.ds(c % width, cyc)] for c in halves], axis=1)

    def twin_copy(i):
        start = pl.multiple_of(i * ROWS, ROWS)
        return remote(contrib.at[1, :, pl.ds(start, ROWS), :], contrib.at[0, :, pl.ds(rows + start, ROWS), :],
                      xsend.at[i], xrecv.at[i], to_dom(1))

    def prep_chunk(i, carry):
        sl = pl.ds(pl.multiple_of(i * ROWS, ROWS), ROWS)
        ctf = ctf_ref[sl, :]
        also = pl.ds(pl.multiple_of(rows + i * ROWS, ROWS), ROWS)

        def apply(a, c, s):
            for b, sign in ((a, 1), (a + angles // 2, -1)):
                x = part_ref[sl, pl.ds(b * lanes, lanes)].astype(F32)
                y = pltpu.roll(x, cyc, 1) * s
                wch[b] = (x * c + y if sign > 0 else x * c - y).astype(BF16)

        for a in range(quarter + 1):
            cx, sx = phase[a, sl, pl.ds(0, lanes)], phase[a, sl, pl.ds(lanes, lanes)]
            cy = phase[quarter - a, also, pl.ds(0, lanes)] * ctf
            sy = phase[quarter - a, also, pl.ds(lanes, lanes)] * ctf
            cc, ss, sc, cs = cx * cy, sx * sy, sx * cy, cx * sy
            apply(a, cc - ss, sc + cs)
            if 0 < a < quarter:
                apply(angles // 2 - a, cc + ss, cs - sc)

        def store(m, re, im):
            first = re.astype(BF16)
            second = jnp.zeros_like(first) if im is None else im.astype(BF16)
            lower = pl.ds(pl.multiple_of(rows + i * ROWS, ROWS), ROWS)
            spec_p[m, sl, pl.ds(0, lanes)] = first
            spec_p[m, sl, pl.ds(lanes, lanes)] = second
            spec_p[m, lower, pl.ds(0, lanes)] = second
            spec_p[m, lower, pl.ds(lanes, lanes)] = -first

        forward_fft(lambda a: wch[a].astype(F32), store, angles)
        rot = rot_ref[sl, :]
        bits_on = [jnp.where((rot & (1 << n)) != 0, 1.0, 0.0).astype(BF16) > 0 for n in range((angles - 1).bit_length())]
        memo = {}

        def staged(level, a):
            a = a % angles
            if (level, a) not in memo:
                if level == 0:
                    memo[level, a] = wch[a]
                else:
                    step = 1 << (level - 1)
                    on = bits_on[level - 1]
                    memo[level, a] = jnp.where(on, staged(level - 1, a + step), staged(level - 1, a))
            return memo[level, a]

        levels = low.bit_length() - 1
        for a in range(angles):
            ych[a] = staged(levels, a)
        for r in range(low):
            line = [ych[r + low * j] for j in range(high)]
            for bit in range((high - 1).bit_length()):
                on = bits_on[levels + bit]
                line = [jnp.where(on, line[(j + (1 << bit)) % high], line[j]) for j in range(high)]
            for j in range(high):
                a = r + low * j
                value = line[j]
                if paired:
                    d = a * lanes // width
                    contrib[parity if d % 2 == 0 else 1 - parity, d // 2, sl, pl.ds(a * lanes % width, lanes)] = value
                elif width % lanes == 0:
                    contrib[a * lanes // width, sl, pl.ds(a * lanes % width, lanes)] = value
                else:
                    for h in range(2):
                        col = a * lanes + h * cyc
                        contrib[col // width, sl, pl.ds(col % width, cyc)] = value[:, h * cyc:(h + 1) * cyc]
        if paired:
            @pl.when(i > 0)
            def _():
                twin_copy(i - 1).start()
        for c in range(chunks):
            if ("prep", c) in plan:
                @pl.when(i == c)
                def _():
                    serve(*plan["prep", c])
        return carry

    lax.fori_loop(0, chunks, prep_chunk, 0)

    spans = [(0, width)]
    if width % lanes == 0 and width // lanes >= 3:
        n = width // lanes
        cuts = [0, n - n // 3 - max(1, n * 2 // 9), n - max(1, n // 6), n]
        spans = [(x * lanes, (y - x) * lanes) for x, y in zip(cuts[:-1], cuts[1:])]

    def contrib_copy(q, c):
        cols = pl.ds(*spans[c])
        return remote(contrib.at[dom ^ q, :, cols], got.at[q, :, cols], asend.at[q, c], arecv.at[q, c], to_dom(q))

    def half_copy(h, c):
        cols = pl.ds(*spans[c])
        return remote(bsend.at[h, :, :, cols], brecv.at[h, :, :, cols], asend.at[h, c], arecv.at[h, c],
                      {"dom": dom ^ first, "cls": zed})

    def joined(c):
        cols = pl.ds(*spans[c])
        return remote(mid.at[:, :, cols], mgot.at[:, :, cols], jsend.at[c], jrecv.at[c], {"dom": dom ^ last, "cls": zed})

    if paired:
        twin_copy(chunks - 1).start()
    else:
        for c in range(len(spans)):
            for q in range(1, D):
                contrib_copy(q, c).start()
        got[0] = contrib[dom]

    for q in range(1, D):
        remote(meta_ref, metas.at[q], msend.at[q], mrecv.at[q], to_dom(q)).wait()
    ids = lax.broadcasted_iota(jnp.int32, (Z * pad, rows), 0)
    gids = lax.broadcasted_iota(jnp.int32, (groups, rows), 0)
    sel_ref[...] = jnp.concatenate([jnp.where(ids == metas[d, pl.ds(0, 1), :], 1.0, 0.0).astype(BF16) for d in range(D)], axis=1)

    def sum_span(c, which=(0, 1, 2, 3)):
        start, size = spans[c]
        cols = pl.ds(start, size)
        for h, chip in enumerate((dom ^ first ^ last, dom ^ first, dom ^ last, dom)):
            if h not in which:
                continue
            sums = jnp.dot(sel_ref[:, pl.ds(0, 2 * rows)], contrib[0, chip // 2, :, cols], preferred_element_type=F32)
            sums = sums.reshape(Z, pad, size)[:, :local, :]
            if h < 2:
                bsend[h, :, :, cols] = sums.astype(BF16)
                half_copy(h, c).start()
            elif h == 2:
                keep[:, pl.ds(0, local), cols] = sums
            else:
                part[:, pl.ds(0, local), cols] = sums

    if paired:
        for i in range(chunks):
            twin_copy(i).wait_recv()
        sum_span(0, (0,))
        serve((0, 2))
        sum_span(0, (1, 2, 3))
        serve((6, 0))
    gsel = jnp.concatenate([jnp.where(gids == metas[d, pl.ds(1, 1), :], 1.0, 0.0).astype(BF16) for d in range(D)], axis=1)
    counts = lax.dot_general(sel_ref[...], gsel, (((1,), (1,)), ((), ())), preferred_element_type=F32)
    wsum = jnp.dot(counts, table * table, precision=lax.Precision.HIGHEST, preferred_element_type=F32)
    wpart[...] = wsum.reshape(Z, pad, wsum.shape[1])

    def w_copy(j):
        return remote(wpart.at[lax.rem(zed + j, Z)], wrecv.at[j], wsend.at[j], wrecv_sem.at[j], to_cls(j))

    for j in range(1, Z):
        w_copy(j).start()

    def s_copy(j, c):
        cols = pl.ds(*spans[c])
        return remote(sbuf.at[lax.rem(zed + j, Z), :, cols], rbuf.at[j, :, cols], ssend.at[j, c], srecv.at[j, c], to_cls(j))

    def send_span(c):
        start, size = spans[c]
        cols = pl.ds(start, size)
        if paired:
            half_copy(1, c).wait_recv()
            joined(c).wait_recv()
            both = brecv[1, :, :, cols].astype(F32) + mgot[:, :, cols].astype(F32)
            part[:, pl.ds(0, local), cols] = part[:, pl.ds(0, local), cols] + both
        else:
            for q in range(1, D):
                contrib_copy(q, c).wait()
            sums = jnp.dot(sel_ref[...], got[:, :, cols].reshape(D * rows, size), preferred_element_type=F32)
            part[:, :, cols] = sums.reshape(Z, pad, size)
        sbuf[:, :, cols] = part[:, pl.ds(0, local), cols].astype(BF16)
        for j in range(1, Z):
            s_copy(j, c).start()

    own.wait()

    def ref_rows(z, slot, start, count):
        sl = pl.ds(start, count)
        out = pl.ds(start, count)

        def store(m, re, im):
            second = jnp.zeros_like(re) if im is None else im
            spec_r[m, slot, out, pl.ds(0, lanes)] = re.astype(BF16)
            spec_r[m, slot, out, pl.ds(lanes, lanes)] = second.astype(BF16)

        forward_fft(lambda a: piece(lambda d: buf.at[d, z], sl, a).astype(F32), store, angles)

    whole = local // ROWS
    rest = local % ROWS

    def pass_on(c):
        start, size = spans[c]
        cols = pl.ds(start, size)
        half_copy(0, c).wait_recv()
        mid[:, :, cols] = (keep[:, pl.ds(0, local), cols] + brecv[0, :, :, cols].astype(F32)).astype(BF16)
        joined(c).start()

    def ref_block(k):
        for q in offsets:
            core_copy(q, origin[k], 1).wait_recv()

        def ref_step(n, carry):
            ref_rows(origin[k], k, pl.multiple_of(n * ROWS, ROWS), ROWS)
            return carry

        lax.fori_loop(0, whole, ref_step, 0)
        if rest:
            ref_rows(origin[k], k, whole * ROWS, rest)

    freqs = angles // 2 + 1
    groups_of = -(-local // 8)
    group = 4
    pieces = freqs // group

    def cross_step(m, lo, hi):
        lhs = spec_r[m, pl.ds(lo, hi - lo)].reshape((hi - lo) * pad, 2 * lanes)
        cross[m, pl.ds(lo * pad, (hi - lo) * pad), :] = lax.dot_general(
            lhs, spec_p[m], (((1,), (1,)), ((), ())), preferred_element_type=F32)

    def crosses(start, end, lo, hi):
        def step(n, carry):
            for g in range(group):
                cross_step(n * group + g, lo, hi)
            return carry

        lax.fori_loop(start, min(end, pieces), step, 0)
        if end > pieces:
            for m in range(pieces * group, freqs):
                cross_step(m, lo, hi)

    def back_step(n, best):
        z, j = n // groups_of, n % groups_of
        start = pl.multiple_of(z * pad + j * 8, 8)

        def load(m, p):
            return cross[m, pl.ds(start, 8), pl.ds(p * rows, rows)]

        top = inverse_max(load, angles)
        row = lax.broadcasted_iota(jnp.int32, (8, rows), 0) + j * 8
        return jnp.maximum(best, jnp.where(row < local, top, -jnp.inf))

    def backs(start, end, best):
        return lax.fori_loop(start, end, back_step, best)

    best = jnp.full((8, rows), -jnp.inf, F32)
    if paired:
        most = (Z - 1) * groups_of
        ref_block(0)
        serve((2, 1), (4, 1))
        sum_span(1)
        serve((0, 3))
        pass_on(0)
        sum_span(2)
        serve((6, 1))
        ref_block(1)
        serve((2, 2), (4, 2), (6, 2))
        ref_block(2)
        crosses(0, pieces // 2, 0, Z - 1)
        send_span(0)
        pass_on(1)
        crosses(pieces // 2, pieces + 1, 0, Z - 1)
        best = backs(0, most // 3, best)
        serve(*[(q, 3) for q in (2, 4, 6)])
        pass_on(2)
        ref_block(Z - 1)
        send_span(1)
        best = backs(most // 3, most, best)
        send_span(2)
        crosses(0, pieces + 1, Z - 1, Z)
        best = backs(most, Z * groups_of, best)
    else:
        for k in range(Z):
            serve(*sorted([(q, k) for q in offsets if q or k], key=lambda e: bin(e[0]).count("1")))
            ref_block(k)
        crosses(0, pieces + 1, 0, Z)
        best = backs(0, Z * groups_of, best)
        for c in range(len(spans)):
            send_span(c)
    best_ref[...] = jnp.max(best, axis=0, keepdims=True) * (1.0 / angles)

    weight = wpart[zed][:local, :]
    for j in range(1, Z):
        w_copy(j).wait()
        weight = weight + wrecv[j][:local, :]
    scale = 1.0 / (jnp.concatenate([weight, weight], axis=1) + tau_reg)
    for c, (start, size) in enumerate(spans):
        cols = pl.ds(start, size)
        total = part[zed, :, cols][:local, :]
        for j in range(1, Z):
            s_copy(j, c).wait()
            total = total + rbuf[j, :, cols].astype(F32)
        new_ref[:, cols] = total * jnp.concatenate([scale] * -(-size // lanes), axis=1)[:, :size]

    if paired:
        for c in range(len(spans)):
            joined(c).wait_send()
            for h in range(2):
                half_copy(h, c).wait_send()
        for i in range(chunks):
            twin_copy(i).wait_send()
    for q in along:
        for o in range(Z):
            @pl.when(jnp.logical_and(o <= zed, zed + 1 < Z))
            def _():
                z_copy(refs_ref, q, o, True).wait_send()

            @pl.when(jnp.logical_and(o >= zed, zed > 0))
            def _():
                z_copy(refs_ref, q, o, False).wait_send()
    for o in range(Z):
        for q in offsets:
            core_copy(q, o, 1).wait_send()
            if q and q not in along:
                plane_copy(q, last_bit(q, 1), o, 1).wait_send()
    if paired:
        plane_copy(D - 2, 2, zed, 0).wait_send()


def per_device(particles, references, owner, class_offset, rotation, shifts, ctf_group, ctf_table):
    D, Z = lax.axis_size("dom"), lax.axis_size("cls")
    groups, cyc = ctf_table.shape
    rows, full = particles.shape
    lanes = 2 * cyc
    angles = full // lanes
    local, width = references.shape
    pad = -(-local // ROWS) * ROWS
    freqs = angles // 2 + 1
    chunks = 3
    dma = pltpu.SemaphoreType.DMA
    paired = D == 8 and Z == 4
    best, new = pl.pallas_call(
        lambda *refs: fused((D, Z, angles, cyc), *refs),
        out_shape=(pltpu.VMEM((1, rows), F32), pltpu.VMEM((local, width), F32)),
        in_specs=[pl.BlockSpec(memory_space=pl.ANY)] * 2 + [pl.BlockSpec(memory_space=pltpu.VMEM)] * 6,
        out_specs=[pl.BlockSpec(memory_space=pltpu.VMEM)] * 2,
        scratch_shapes=[
            pltpu.VMEM((rows, full), BF16),
            pltpu.VMEM((angles // 4 + 1, 3 * SPAN, 2 * lanes), BF16),
            pltpu.VMEM((angles // 4 + 1, 2 * rows, 2 * lanes), F32),
            pltpu.VMEM((rows, lanes), F32),
            pltpu.VMEM((rows, lanes), jnp.int32),
            pltpu.VMEM((8, rows), jnp.int32),
            pltpu.VMEM((D, Z, local, width), BF16),
            pltpu.VMEM((angles, ROWS, lanes), BF16),
            pltpu.VMEM((angles, ROWS, lanes), BF16),
            pltpu.VMEM((freqs, 2 * rows, 2 * lanes), BF16),
            pltpu.VMEM((freqs, Z, pad, 2 * lanes), BF16),
            pltpu.VMEM((freqs, Z * pad, 2 * rows), F32),
            pltpu.VMEM((2, D // 2, 2 * rows, width) if paired else (D, rows, width), BF16),
            pltpu.VMEM((1, ROWS, lanes) if paired else (D, rows, width), BF16),
            pltpu.VMEM((D, 8, rows), jnp.int32),
            pltpu.VMEM((Z, pad, width), F32),
            pltpu.VMEM((Z, pad, cyc), F32),
            pltpu.VMEM((Z, local, width), BF16),
            pltpu.VMEM((Z, local, width), BF16),
            pltpu.VMEM((Z, pad, cyc), F32),
            pltpu.VMEM((Z * pad, D * rows), BF16),
            pltpu.VMEM((Z, pad, width) if paired else (1, 8, lanes), F32),
            pltpu.VMEM((2, Z, local, width) if paired else (1, 1, ROWS, lanes), BF16),
            pltpu.VMEM((2, Z, local, width) if paired else (1, 1, ROWS, lanes), BF16),
            pltpu.VMEM((Z, local, width), BF16),
            pltpu.VMEM((Z, local, width), BF16),
            dma((chunks,)), dma((chunks,)),
            dma, dma, dma((2, 2, Z)), dma((2, Z)),
            dma((D // 2, Z)), dma((D // 2, Z)), dma((D // 2, Z)), dma((D // 2, Z)),
            dma((D, chunks)), dma((D, chunks)), dma((D,)), dma((D,)),
            dma((Z, chunks)), dma((Z, chunks)), dma((Z,)), dma((Z,)),
            dma((rows // ROWS,)), dma((rows // ROWS,)),
        ],
        compiler_params=pltpu.CompilerParams(collective_id=0, has_side_effects=True,
                                             vmem_limit_bytes=60 << 20),
        name="class_pass",
    )(particles, references, shifts.T, rotation[None], owner.T, class_offset[None], ctf_group[None], ctf_table)
    return best[0], new


def solution(mesh):
    return jax.shard_map(
        per_device,
        mesh=mesh,
        in_specs=(
            P(("dom", "cls"), None),
            P("cls", "dom"),
            P(("dom", "cls"), None),
            P(("dom", "cls")),
            P(("dom", "cls")),
            P(("dom", "cls"), None),
            P(("dom", "cls")),
            P(),
        ),
        out_specs=(P(("dom", "cls")), P("cls", "dom")),
        check_vma=False,
    )
```

```python
import math

import jax
import jax.numpy as jnp
from jax import lax
from jax.experimental import pallas as pl
from jax.experimental.pallas import tpu as pltpu
from jax.sharding import PartitionSpec as P

BOX = 128
SPAN = 16
EARLY = -0.5
tau_reg = 1.0
ROWS = 16
F32 = jnp.float32
BF16 = jnp.bfloat16
MESH = pl.DeviceIdType.MESH


def split_angles(angles):
    even = angles & -angles
    return even, angles // even


def lin(terms):
    total = None
    for factor, value in terms:
        if value is None or abs(factor) < 1e-12:
            continue
        if total is None:
            total = value if abs(factor - 1) < 1e-12 else (-value if abs(factor + 1) < 1e-12 else value * factor)
        elif abs(factor - 1) < 1e-12:
            total = total + value
        elif abs(factor + 1) < 1e-12:
            total = total - value
        else:
            total = total + value * factor
    return total


def add(a, b):
    return b if a is None else (a if b is None else a + b)


def sub(a, b):
    if b is None:
        return a
    return -b if a is None else a - b


def turn(re, im, part, whole):
    if part == 0:
        return re, im
    c, s = math.cos(2 * math.pi * part / whole), math.sin(2 * math.pi * part / whole)
    return lin([(c, re), (-s, im)]), lin([(s, re), (c, im)])


def three(a, b, c, sign):
    tr, ti = add(b[0], c[0]), add(b[1], c[1])
    er, ei = lin([(sign * math.sqrt(0.75), sub(b[0], c[0]))]), None
    if b[1] is not None or c[1] is not None:
        ei = lin([(sign * math.sqrt(0.75), sub(b[1], c[1]))])
    mr = sub(a[0], lin([(0.5, tr)]))
    mi = None if ti is None and a[1] is None else sub(a[1], lin([(0.5, ti)]))
    first = (add(a[0], tr), None if a[1] is None and ti is None else add(a[1], ti))
    second = (mr if ei is None else mr - ei, add(mi, er))
    third = (mr if ei is None else mr + ei, -er if mi is None else mi - er)
    return first, second, third


def nine_dft(values, sign, wanted):
    inner = [three(values[j], values[j + 3], values[j + 6], sign) for j in range(3)]
    out = {}
    for k in range(3):
        row = [turn(*inner[j][k], sign * j * k, 9) for j in range(3)]
        for l, x in enumerate(three(*row, sign)):
            out[k + 3 * l] = x
    return {k: out[k] for k in out if k in wanted}


def odd_dft(values, sign, wanted):
    n = len(values)
    if n == 9:
        return nine_dft(values, sign, wanted)
    half = n // 2
    sums = [(add(values[j][0], values[n - j][0]), add(values[j][1], values[n - j][1])) for j in range(1, half + 1)]
    diffs = [(sub(values[j][0], values[n - j][0]), sub(values[j][1], values[n - j][1])) for j in range(1, half + 1)]
    out = {}
    for k in range(half + 1):
        pair = [x for x in (k, n - k) if x in wanted]
        if not pair:
            continue
        cs = [math.cos(2 * math.pi * ((j * k) % n) / n) for j in range(1, half + 1)]
        sn = [sign * math.sin(2 * math.pi * ((j * k) % n) / n) for j in range(1, half + 1)]
        even_re = lin([(1.0, values[0][0])] + [(c, s[0]) for c, s in zip(cs, sums)])
        even_im = lin([(1.0, values[0][1])] + [(c, s[1]) for c, s in zip(cs, sums)])
        odd_re = lin([(-s, d[1]) for s, d in zip(sn, diffs)])
        odd_im = lin([(s, d[0]) for s, d in zip(sn, diffs)])
        for x in pair:
            if x == k:
                out[x] = (add(even_re, odd_re), add(even_im, odd_im))
            else:
                out[x] = (sub(even_re, odd_re), sub(even_im, odd_im))
    return out


def real_eight_dft(v):
    r = math.sqrt(0.5)
    s = [v[j] + v[j + 4] for j in range(4)]
    d = [v[j] - v[j + 4] for j in range(4)]
    a, b = s[0] + s[2], s[1] + s[3]
    p, q = r * (d[1] - d[3]), r * (d[1] + d[3])
    return [(a + b, None), (d[0] + p, -d[2] - q), (s[0] - s[2], s[3] - s[1]), (d[0] - p, d[2] - q), (a - b, None)]


def real_even_dft(values):
    n = len(values)
    if n == 8:
        return real_eight_dft(values)
    half = n // 2
    sums = [add(values[j], values[n - j]) for j in range(1, half)]
    diffs = [sub(values[j], values[n - j]) for j in range(1, half)]
    plus, minus = values[0] + values[half], values[0] - values[half]
    out = []
    for k in range(half + 1):
        cs = [math.cos(2 * math.pi * j * k / n) for j in range(1, half)]
        sn = [math.sin(2 * math.pi * j * k / n) for j in range(1, half)]
        re = lin([(1.0, minus if k % 2 else plus)] + list(zip(cs, sums)))
        im = lin([(-s, d) for s, d in zip(sn, diffs)]) if 0 < k < half else None
        out.append((re, im))
    return out


def forward_fft(load, store, angles):
    n1, n2 = split_angles(angles)
    inner = [real_even_dft([load(n2 * i + j) for i in range(n1)]) for j in range(n2)]
    for k1 in range(n1 // 2 + 1):
        values = [turn(*inner[j][k1], -((j * k1) % angles), angles) for j in range(n2)]
        for k2 in range(n2):
            pass
        wanted = set(range(n2)) if 0 < k1 < n1 // 2 else set(range(n2 // 2 + 1))
        for k2, (re, im) in odd_dft(values, -1.0, wanted).items():
            m = k1 + n1 * k2
            if m > angles // 2:
                m, im = angles - m, (None if im is None else -im)
            store(m, re, im)


def inverse_max(load, angles):
    n1, n2 = split_angles(angles)

    def value(m):
        if m == 0 or m == angles // 2:
            return load(m, 0), None
        if m > angles // 2:
            re, im = load(angles - m, 0), load(angles - m, 1)
            return re, -im
        return load(m, 0), load(m, 1)

    grid = []
    for k1 in range(n1 // 2 + 1):
        values = [value((k1 + n1 * k2) % angles) for k2 in range(n2)]
        got = odd_dft(values, 1.0, set(range(n2)))
        row = []
        for j in range(n2):
            row.append(turn(*got[j], (j * k1) % angles, angles))
        grid.append(row)
    best = None
    half = n1 // 2
    for j in range(n2):
        h0, h4 = grid[0][j][0], grid[half][j][0]
        if n1 == 8:
            r = math.sqrt(2.0)
            (a1, b1), (a2, b2), (a3, b3) = grid[1][j], grid[2][j], grid[3][j]
            plus, minus = h0 + h4, h0 - h4
            twice, sine = 2.0 * a2, 2.0 * b2
            w, e = r * (a1 - a3), r * (b1 + b3)
            tops = [plus + twice + 2.0 * jnp.abs(a1 + a3), plus - twice + 2.0 * jnp.abs(b1 - b3),
                    minus + w + jnp.abs(e + sine), minus - w + jnp.abs(e - sine)]
            for top in tops:
                best = top if best is None else jnp.maximum(best, top)
            continue
        plus, minus = h0 + h4, h0 - h4
        doubled = [(2.0 * grid[k][j][0], 2.0 * grid[k][j][1]) for k in range(1, half)]
        for i in range(half + 1):
            even = lin([(1.0, minus if i % 2 else plus)] + [(math.cos(2 * math.pi * i * (k + 1) / n1), doubled[k][0]) for k in range(half - 1)])
            odd = lin([(-math.sin(2 * math.pi * i * (k + 1) / n1), doubled[k][1]) for k in range(half - 1)]) if 0 < i < half else None
            top = even if odd is None else even + jnp.abs(odd)
            best = top if best is None else jnp.maximum(best, top)
    return best


def sin_cos_turns(u):
    u = u - jnp.floor(u + 0.5)
    v = (u * u) * (4 * math.pi * math.pi)
    s = jnp.full_like(v, 1.0 / math.factorial(17))
    for k in (15, 13, 11, 9, 7, 5, 3, 1):
        s = s * v + ((-1.0) ** (k // 2)) / math.factorial(k)
    c = jnp.full_like(v, -1.0 / math.factorial(18))
    for k in (16, 14, 12, 10, 8, 6, 4, 2, 0):
        c = c * v + ((-1.0) ** (k // 2)) / math.factorial(k)
    return s * (u * (2 * math.pi)), c


def fused(dims, part_hbm, refs_ref, shift_ref, turn_ref, owner_ref, offset_ref, group_ref, table_ref,
          best_ref, new_ref,
          part_ref, tab, phase, ctf_ref, rot_ref, meta_ref, buf, wch, ych, spec_p, spec_r, cross, contrib, got, metas, part, wpart, sbuf, rbuf, wrecv, sel_ref, keep, bsend, brecv, mid, mgot, jsend, jrecv,
          part_sem, own_sem, zsend, zrecv, psend, precv, csend, crecv, asend, arecv, msend, mrecv,
          ssend, srecv, wsend, wrecv_sem, xsend, xrecv):
    D, Z, angles, cyc = dims
    dom, zed = lax.axis_index("dom"), lax.axis_index("cls")
    rows, lanes = part_ref.shape[0], 2 * cyc
    local, width = refs_ref.shape
    pad = part.shape[1]
    bits = [1 << i for i in range(1, D.bit_length() - 1)]
    offsets = list(range(0, D, 2))
    paired = len(bits) == 2 and Z == 4
    parity = lax.rem(dom, 2)
    last, first = 2 + 2 * parity, 4 - 2 * parity
    along = [0, D - 2] if paired else [0]

    def to_dom(q):
        return {"dom": dom ^ q, "cls": zed}

    def to_cls(j):
        return {"dom": dom, "cls": lax.rem(zed + j, Z)}

    near_first = [sorted(range(Z), key=lambda o: (abs(o - z), o)) for z in range(Z)]
    origin = [sum(jnp.where(zed == z, near_first[z][k], 0) for z in range(Z)) for k in range(Z)]

    def remote(src, dst, s, r, where):
        return pltpu.make_async_remote_copy(src_ref=src, dst_ref=dst, send_sem=s, recv_sem=r,
                                            device_id=where, device_id_type=MESH)

    def block(q, o):
        return buf.at[dom ^ q, o]

    def z_copy(src, q, o, up):
        to = {"dom": dom, "cls": zed + 1 if up else zed - 1}
        line = along.index(q)
        return remote(src, buf.at[dom ^ q, o], zsend.at[1 if up else 0, line, o], zrecv.at[line, o], to)

    def z_pass(src, q, o, moving_up, moving_down):
        @pl.when(jnp.logical_and(moving_up, zed + 1 < Z))
        def _():
            z_copy(src, q, o, True).start()

        @pl.when(jnp.logical_and(moving_down, zed > 0))
        def _():
            z_copy(src, q, o, False).start()

    def source(q, o, h):
        return refs_ref if q == 0 and h == 0 else block(q, o)

    def plane_copy(child, bit, o, h):
        q = child ^ bit
        return remote(source(q, o, h), block(q, o), psend.at[child // 2, o], precv.at[child // 2, o], to_dom(bit))

    def core_copy(q, o, h):
        return remote(source(q, o, h), block(q, o), csend, crecv.at[q // 2, o], to_dom(1))

    def last_bit(q, h):
        return (1 << (q.bit_length() - 1)) if h % 2 == 0 else (q & -q)

    def at_hops(h, act):
        if h == 0:
            act(zed, 0)
            return
        for side in (1, -1):
            o = zed + side * h

            @pl.when(jnp.logical_and(o >= 0, o < Z))
            def _():
                act(o, side)

    fetch = pltpu.make_async_copy(part_hbm, part_ref, part_sem)
    fetch.start()
    barrier = pltpu.get_barrier_semaphore()
    for q in range(1, D):
        pl.semaphore_signal(barrier, inc=1, device_id=to_dom(q), device_id_type=MESH)
    for j in range(1, Z):
        pl.semaphore_signal(barrier, inc=1, device_id=to_cls(j), device_id_type=MESH)
    meta_ref[...] = jnp.zeros_like(meta_ref)
    meta_ref[pl.ds(0, 1), :] = owner_ref[...] * pad + offset_ref[...]
    meta_ref[pl.ds(1, 1), :] = group_ref[...]
    def column(row):
        return jnp.transpose(jnp.broadcast_to(row.astype(F32), (lanes, rows)))

    quarter, levels = angles // 4, tab.shape[1] // SPAN
    left = lax.broadcasted_iota(jnp.int32, (SPAN, lanes), 1) < cyc
    radius = (lax.rem(lax.broadcasted_iota(jnp.int32, (SPAN, lanes), 1), cyc) + 1).astype(F32) / BOX
    radius = radius * (lax.broadcasted_iota(jnp.int32, (SPAN, lanes), 0) - SPAN // 2).astype(F32)
    for a in range(quarter + 1):
        s, c = sin_cos_turns(radius * (math.cos(2 * math.pi * a / angles) if a < quarter else 0.0))
        for h, value in enumerate((c, jnp.where(left, -s, s))):
            for n in range(levels):
                tab[a, pl.ds(n * SPAN, SPAN), pl.ds(h * lanes, lanes)] = value.astype(BF16)
                value = value - value.astype(BF16).astype(F32)
    moved = jnp.concatenate([column(shift_ref[pl.ds(n, 1), :]) for n in range(2)], axis=0).astype(jnp.int32)
    steps = lax.rem(lax.broadcasted_iota(jnp.int32, (2 * rows, levels * SPAN), 1), SPAN) - SPAN // 2
    picked = jnp.where(moved[:, :levels * SPAN] == steps, 1.0, 0.0).astype(BF16)
    for a in range(quarter + 1):
        phase[a] = jnp.dot(picked, tab[a], preferred_element_type=F32)
    rot_ref[...] = column(turn_ref[...]).astype(jnp.int32)
    groups = table_ref.shape[0]
    table = table_ref[...]
    gcol = column(group_ref[...]).astype(jnp.int32)
    gcol = jnp.concatenate([gcol] * -(-groups // lanes), axis=1)[:, :groups]
    pick = jnp.where(gcol == lax.broadcasted_iota(jnp.int32, (rows, groups), 1), 1.0, 0.0)
    one = jnp.dot(pick, table, precision=lax.Precision.HIGHEST, preferred_element_type=F32)
    ctf_ref[...] = jnp.concatenate([one, one], axis=1)

    pl.semaphore_wait(barrier, D + Z - 2)

    own = pltpu.make_async_copy(refs_ref, buf.at[dom, zed], own_sem)
    own.start()
    z_pass(refs_ref, 0, zed, zed >= 0, zed >= 0)

    def children(q, h):
        return [(q ^ b, b) for b in bits if not q & b and last_bit(q ^ b, h) == b]

    def event(q, h, only=None):
        def act(o, side):
            if only == "plane":
                pass
            elif h and q in along:
                z_copy(refs_ref, q, o, True).wait_recv()
                if side < 0:
                    z_pass(block(q, o), q, o, zed >= 0, zed < 0)
                else:
                    z_pass(block(q, o), q, o, zed < 0, zed >= 0)
            elif q:
                plane_copy(q, last_bit(q, h), o, h).wait_recv()
                if q in along:
                    z_pass(block(q, o), q, o, zed >= 0, zed >= 0)
            if only == "line":
                return
            if not paired or q == 0:
                for child, b in children(q, h):
                    if not paired or child not in along:
                        plane_copy(child, b, o, h).start()
            elif h == 0 and q not in along:
                @pl.when(first == D - 2 - q)
                def _():
                    plane_copy(D - 2, D - 2 - q, o, h).start()
            core_copy(q, o, h).start()

        at_hops(h, act)

    event(0, 0)
    for q in range(1, D):
        remote(meta_ref, metas.at[q], msend, mrecv, to_dom(q)).start()
    metas[0] = meta_ref[...]

    plan = {("prep", 6): [(0, 1, "line"), (2, 0), (4, 0), (0, 1, "plane")]} if paired else {}

    def serve(*pairs):
        for q, h, *part_of in pairs:
            if h < Z:
                event(q, h, *part_of)

    fetch.wait()
    chunks = rows // ROWS
    low, high = split_angles(angles)

    def piece(ref, sl, a):
        if width % lanes == 0:
            return ref(a * lanes // width)[sl, pl.ds(a * lanes % width, lanes)]
        halves = [(a * lanes + h * cyc) for h in range(2)]
        return jnp.concatenate([ref(c // width)[sl, pl.ds(c % width, cyc)] for c in halves], axis=1)

    def twin_copy(i):
        start = pl.multiple_of(i * ROWS, ROWS)
        return remote(contrib.at[1, :, pl.ds(start, ROWS), :], contrib.at[0, :, pl.ds(rows + start, ROWS), :],
                      xsend, xrecv, to_dom(1))

    def prep_chunk(i, carry):
        sl = pl.ds(pl.multiple_of(i * ROWS, ROWS), ROWS)
        ctf = ctf_ref[sl, :]
        also = pl.ds(pl.multiple_of(rows + i * ROWS, ROWS), ROWS)

        def apply(a, c, s):
            for b, sign in ((a, 1), (a + angles // 2, -1)):
                x = part_ref[sl, pl.ds(b * lanes, lanes)].astype(F32)
                y = pltpu.roll(x, cyc, 1) * s
                wch[b] = (x * c + y if sign > 0 else x * c - y).astype(BF16)

        for a in range(quarter + 1):
            cx, sx = phase[a, sl, pl.ds(0, lanes)], phase[a, sl, pl.ds(lanes, lanes)]
            cy = phase[quarter - a, also, pl.ds(0, lanes)] * ctf
            sy = phase[quarter - a, also, pl.ds(lanes, lanes)] * ctf
            cc, ss, sc, cs = cx * cy, sx * sy, sx * cy, cx * sy
            apply(a, cc - ss, sc + cs)
            if 0 < a < quarter:
                apply(angles // 2 - a, cc + ss, cs - sc)

        def store(m, re, im):
            first = re.astype(BF16)
            second = jnp.zeros_like(first) if im is None else im.astype(BF16)
            lower = pl.ds(pl.multiple_of(rows + i * ROWS, ROWS), ROWS)
            spec_p[m, sl, pl.ds(0, lanes)] = first
            spec_p[m, sl, pl.ds(lanes, lanes)] = second
            spec_p[m, lower, pl.ds(0, lanes)] = second
            spec_p[m, lower, pl.ds(lanes, lanes)] = -first

        forward_fft(lambda a: wch[a].astype(F32), store, angles)
        rot = rot_ref[sl, :]
        bits_on = [jnp.where((rot & (1 << n)) != 0, 1.0, 0.0).astype(BF16) > 0 for n in range((angles - 1).bit_length())]
        memo = {}

        def staged(level, a):
            a = a % angles
            if (level, a) not in memo:
                if level == 0:
                    memo[level, a] = wch[a]
                else:
                    step = 1 << (level - 1)
                    on = bits_on[level - 1]
                    memo[level, a] = jnp.where(on, staged(level - 1, a + step), staged(level - 1, a))
            return memo[level, a]

        levels = low.bit_length() - 1
        for a in range(angles):
            ych[a] = staged(levels, a)
        for r in range(low):
            line = [ych[r + low * j] for j in range(high)]
            for bit in range((high - 1).bit_length()):
                on = bits_on[levels + bit]
                line = [jnp.where(on, line[(j + (1 << bit)) % high], line[j]) for j in range(high)]
            for j in range(high):
                a = r + low * j
                value = line[j]
                if paired:
                    d = a * lanes // width
                    contrib[parity if d % 2 == 0 else 1 - parity, d // 2, sl, pl.ds(a * lanes % width, lanes)] = value
                elif width % lanes == 0:
                    contrib[a * lanes // width, sl, pl.ds(a * lanes % width, lanes)] = value
                else:
                    for h in range(2):
                        col = a * lanes + h * cyc
                        contrib[col // width, sl, pl.ds(col % width, cyc)] = value[:, h * cyc:(h + 1) * cyc]
        if paired:
            @pl.when(i > 0)
            def _():
                twin_copy(i - 1).start()
        for c in range(chunks):
            if ("prep", c) in plan:
                @pl.when(i == c)
                def _():
                    serve(*plan["prep", c])
        return carry

    lax.fori_loop(0, chunks, prep_chunk, 0)

    spans = [(0, width)]
    if width % lanes == 0 and width // lanes >= 3:
        n = width // lanes
        last_cut, next_cut = n - max(1, n // 9), n - max(1, n // 9) - max(1, 2 * n // 9)
        cuts = [0, (next_cut + 1) // 2, next_cut, last_cut, n]
        spans = [(x * lanes, (y - x) * lanes) for x, y in zip(cuts[:-1], cuts[1:])]

    def contrib_copy(q, c):
        cols = pl.ds(*spans[c])
        return remote(contrib.at[dom ^ q, :, cols], got.at[q, :, cols], asend.at[q, c], arecv.at[q, c], to_dom(q))

    def half_copy(h, c):
        cols = pl.ds(*spans[c])
        return remote(bsend.at[h, :, :, cols], brecv.at[h, :, :, cols], asend.at[0, 0], arecv.at[h, c],
                      {"dom": dom ^ first, "cls": zed})

    def joined(c):
        cols = pl.ds(*spans[c])
        return remote(mid.at[:, :, cols], mgot.at[:, :, cols], jsend, jrecv.at[c], {"dom": dom ^ last, "cls": zed})

    if paired:
        twin_copy(chunks - 1).start()
    else:
        for c in range(len(spans)):
            for q in range(1, D):
                contrib_copy(q, c).start()
        got[0] = contrib[dom]

    others = metas.at[pl.ds(1, D - 1)]
    remote(others, others, msend, mrecv, to_dom(1)).wait()
    ids = lax.broadcasted_iota(jnp.int32, (Z * pad, rows), 0)
    gids = lax.broadcasted_iota(jnp.int32, (groups, rows), 0)
    sel_ref[...] = jnp.concatenate([jnp.where(ids == metas[d, pl.ds(0, 1), :], 1.0, 0.0).astype(BF16) for d in range(D)], axis=1)

    def sum_span(c, which=(0, 1, 2, 3)):
        start, size = spans[c]
        cols = pl.ds(start, size)
        for h, chip in enumerate((dom ^ first ^ last, dom ^ first, dom ^ last, dom)):
            if h not in which:
                continue
            sums = jnp.dot(sel_ref[:, pl.ds(0, 2 * rows)], contrib[0, chip // 2, :, cols], preferred_element_type=F32)
            sums = sums.reshape(Z, pad, size)[:, :local, :]
            if h < 2:
                bsend[h, :, :, cols] = sums.astype(BF16)
                half_copy(h, c).start()
            elif h == 2:
                keep[:, pl.ds(0, local), cols] = sums
            else:
                part[:, pl.ds(0, local), cols] = sums

    if paired:
        twin_all = remote(contrib.at[1, :, pl.ds(0, rows), :], contrib.at[0, :, pl.ds(rows, rows), :], xsend, xrecv, to_dom(1))
        twin_all.wait_recv()
        sum_span(0)
    gsel = jnp.concatenate([jnp.where(gids == metas[d, pl.ds(1, 1), :], 1.0, 0.0).astype(BF16) for d in range(D)], axis=1)
    counts = lax.dot_general(sel_ref[...], gsel, (((1,), (1,)), ((), ())), preferred_element_type=F32)
    wsum = jnp.dot(counts, table * table, precision=lax.Precision.HIGHEST, preferred_element_type=F32)
    wpart[...] = wsum.reshape(Z, pad, wsum.shape[1])

    def w_copy(j):
        return remote(wpart.at[lax.rem(zed + j, Z)], wrecv.at[j], wsend, wrecv_sem, to_cls(j))

    for j in range(1, Z):
        w_copy(j).start()

    def s_copy(j, c):
        cols = pl.ds(*spans[c])
        return remote(sbuf.at[lax.rem(zed + j, Z), :, cols], rbuf.at[j, :, cols], ssend, srecv.at[c], to_cls(j))

    def send_span(c):
        start, size = spans[c]
        cols = pl.ds(start, size)
        if paired:
            half_copy(1, c).wait_recv()
            joined(c).wait_recv()
            both = brecv[1, :, :, cols].astype(F32) + mgot[:, :, cols].astype(F32)
            part[:, pl.ds(0, local), cols] = part[:, pl.ds(0, local), cols] + both
        else:
            for q in range(1, D):
                contrib_copy(q, c).wait()
            sums = jnp.dot(sel_ref[...], got[:, :, cols].reshape(D * rows, size), preferred_element_type=F32)
            part[:, :, cols] = sums.reshape(Z, pad, size)
        sbuf[:, :, cols] = part[:, pl.ds(0, local), cols].astype(BF16)
        for j in range(1, Z):
            s_copy(j, c).start()

    if paired:
        serve((0, 2), (6, 0))
    own.wait()

    def ref_rows(z, slot, start, count):
        sl = pl.ds(start, count)
        out = pl.ds(start, count)

        def store(m, re, im):
            second = jnp.zeros_like(re) if im is None else im
            spec_r[m, slot, out, pl.ds(0, lanes)] = re.astype(BF16)
            spec_r[m, slot, out, pl.ds(lanes, lanes)] = second.astype(BF16)

        forward_fft(lambda a: piece(lambda d: buf.at[d, z], sl, a).astype(F32), store, angles)

    whole = local // ROWS
    rest = local % ROWS

    def pass_on(c):
        start, size = spans[c]
        cols = pl.ds(start, size)
        half_copy(0, c).wait_recv()
        mid[:, :, cols] = (keep[:, pl.ds(0, local), cols] + brecv[0, :, :, cols].astype(F32)).astype(BF16)
        joined(c).start()

    def ref_block(k):
        for q in offsets:
            core_copy(q, origin[k], 1).wait_recv()

        def ref_step(n, carry):
            ref_rows(origin[k], k, pl.multiple_of(n * ROWS, ROWS), ROWS)
            return carry

        lax.fori_loop(0, whole, ref_step, 0)
        if rest:
            ref_rows(origin[k], k, whole * ROWS, rest)

    freqs = angles // 2 + 1
    groups_of = -(-local // 8)
    group = 4
    pieces = freqs // group

    def cross_step(m, lo, hi):
        lhs = spec_r[m, pl.ds(lo, hi - lo)].reshape((hi - lo) * pad, 2 * lanes)
        cross[m, pl.ds(lo * pad, (hi - lo) * pad), :] = lax.dot_general(
            lhs, spec_p[m], (((1,), (1,)), ((), ())), preferred_element_type=F32)

    def crosses(start, end, lo, hi):
        def step(n, carry):
            for g in range(group):
                cross_step(n * group + g, lo, hi)
            return carry

        lax.fori_loop(start, min(end, pieces), step, 0)
        if end > pieces:
            for m in range(pieces * group, freqs):
                cross_step(m, lo, hi)

    def back_step(n, best):
        z, j = n // groups_of, n % groups_of
        start = pl.multiple_of(z * pad + j * 8, 8)

        def load(m, p):
            return cross[m, pl.ds(start, 8), pl.ds(p * rows, rows)]

        top = inverse_max(load, angles)
        row = lax.broadcasted_iota(jnp.int32, (8, rows), 0) + j * 8
        return jnp.maximum(best, jnp.where(row < local, top, -jnp.inf))

    def backs(start, end, best):
        return lax.fori_loop(start, end, back_step, best)

    best = jnp.full((8, rows), -jnp.inf, F32)
    if paired:
        mid_z, all_z = Z // 2, Z * groups_of
        most = mid_z * groups_of
        ref_block(0)
        serve((2, 1), (4, 1))
        sum_span(1)
        serve((0, 3))
        pass_on(0)
        for c in range(2, len(spans)):
            sum_span(c)
        serve((6, 1))
        ref_block(1)
        crosses(0, pieces + 1, 0, mid_z)
        serve((2, 2), (4, 2), (6, 2))
        send_span(0)
        pass_on(1)
        ref_block(2)
        best = backs(0, most, best)
        pass_on(2)
        serve(*[(q, 3) for q in (2, 4, 6)])
        send_span(1)
        pass_on(3)
        ref_block(Z - 1)
        crosses(0, pieces // 2, mid_z, Z)
        send_span(2)
        crosses(pieces // 2, pieces + 1, mid_z, Z)
        send_span(3)
        best = backs(most, all_z, best)
    else:
        for k in range(Z):
            serve(*sorted([(q, k) for q in offsets if q or k], key=lambda e: bin(e[0]).count("1")))
            ref_block(k)
        crosses(0, pieces + 1, 0, Z)
        best = backs(0, Z * groups_of, best)
        for c in range(len(spans)):
            send_span(c)
    best_ref[...] = jnp.max(best, axis=0, keepdims=True) * (1.0 / angles)

    weight = wpart[zed][:local, :]
    w_all = wrecv.at[pl.ds(1, Z - 1)]
    remote(w_all, w_all, wsend, wrecv_sem, to_cls(1)).wait()
    for j in range(1, Z):
        weight = weight + wrecv[j][:local, :]
    scale = 1.0 / (jnp.concatenate([weight, weight], axis=1) + tau_reg)
    for c, (start, size) in enumerate(spans):
        cols = pl.ds(start, size)
        total = part[zed, :, cols][:local, :]
        got_all = rbuf.at[pl.ds(1, Z - 1), :, cols]
        remote(got_all, got_all, ssend, srecv.at[c], to_cls(1)).wait_recv()
        for j in range(1, Z):
            total = total + rbuf[j, :, cols].astype(F32)
        new_ref[:, cols] = total * jnp.concatenate([scale] * -(-size // lanes), axis=1)[:, :size]

    remote(sbuf.at[pl.ds(0, Z - 1)], sbuf.at[pl.ds(0, Z - 1)], ssend, srecv.at[0], to_cls(1)).wait_send()
    if paired:
        remote(mid, mgot, jsend, jrecv.at[0], to_dom(1)).wait_send()
        remote(bsend, brecv, asend.at[0, 0], arecv.at[0, 0], to_dom(1)).wait_send()
        twin_all.wait_send()
    for q in along:
        for o in range(Z):
            @pl.when(jnp.logical_and(o <= zed, zed + 1 < Z))
            def _():
                z_copy(refs_ref, q, o, True).wait_send()

            @pl.when(jnp.logical_and(o >= zed, zed > 0))
            def _():
                z_copy(refs_ref, q, o, False).wait_send()
    remote(buf.at[pl.ds(0, D // 2)], buf.at[pl.ds(0, D // 2)], csend, crecv.at[0, 0], to_dom(1)).wait_send()
    for o in range(Z):
        for q in offsets:
            if q and q not in along:
                plane_copy(q, last_bit(q, 1), o, 1).wait_send()
    if paired:
        plane_copy(D - 2, 2, zed, 0).wait_send()


def per_device(particles, references, owner, class_offset, rotation, shifts, ctf_group, ctf_table):
    D, Z = lax.axis_size("dom"), lax.axis_size("cls")
    groups, cyc = ctf_table.shape
    rows, full = particles.shape
    lanes = 2 * cyc
    angles = full // lanes
    local, width = references.shape
    pad = -(-local // ROWS) * ROWS
    freqs = angles // 2 + 1
    chunks = 4
    dma = pltpu.SemaphoreType.DMA
    paired = D == 8 and Z == 4
    best, new = pl.pallas_call(
        lambda *refs: fused((D, Z, angles, cyc), *refs),
        out_shape=(pltpu.VMEM((1, rows), F32), pltpu.VMEM((local, width), F32)),
        in_specs=[pl.BlockSpec(memory_space=pl.ANY)] * 2 + [pl.BlockSpec(memory_space=pltpu.VMEM)] * 6,
        out_specs=[pl.BlockSpec(memory_space=pltpu.VMEM)] * 2,
        scratch_shapes=[
            pltpu.VMEM((rows, full), BF16),
            pltpu.VMEM((angles // 4 + 1, 3 * SPAN, 2 * lanes), BF16),
            pltpu.VMEM((angles // 4 + 1, 2 * rows, 2 * lanes), F32),
            pltpu.VMEM((rows, lanes), F32),
            pltpu.VMEM((rows, lanes), jnp.int32),
            pltpu.VMEM((8, rows), jnp.int32),
            pltpu.VMEM((D, Z, local, width), BF16),
            pltpu.VMEM((angles, ROWS, lanes), BF16),
            pltpu.VMEM((angles, ROWS, lanes), BF16),
            pltpu.VMEM((freqs, 2 * rows, 2 * lanes), BF16),
            pltpu.VMEM((freqs, Z, pad, 2 * lanes), BF16),
            pltpu.VMEM((freqs, Z * pad, 2 * rows), F32),
            pltpu.VMEM((2, D // 2, 2 * rows, width) if paired else (D, rows, width), BF16),
            pltpu.VMEM((1, ROWS, lanes) if paired else (D, rows, width), BF16),
            pltpu.VMEM((D, 8, rows), jnp.int32),
            pltpu.VMEM((Z, pad, width), F32),
            pltpu.VMEM((Z, pad, cyc), F32),
            pltpu.VMEM((Z, local, width), BF16),
            pltpu.VMEM((Z, local, width), BF16),
            pltpu.VMEM((Z, pad, cyc), F32),
            pltpu.VMEM((Z * pad, D * rows), BF16),
            pltpu.VMEM((Z, pad, width) if paired else (1, 8, lanes), F32),
            pltpu.VMEM((2, Z, local, width) if paired else (1, 1, ROWS, lanes), BF16),
            pltpu.VMEM((2, Z, local, width) if paired else (1, 1, ROWS, lanes), BF16),
            pltpu.VMEM((Z, local, width), BF16),
            pltpu.VMEM((Z, local, width), BF16),
            dma, dma((chunks,)),
            dma, dma, dma((2, 2, Z)), dma((2, Z)),
            dma((D // 2, Z)), dma((D // 2, Z)), dma, dma((D // 2, Z)),
            dma((1, 1) if paired else (D, chunks)), dma((2 if paired else D, chunks)), dma, dma,
            dma, dma((chunks,)), dma, dma, dma, dma,
        ],
        compiler_params=pltpu.CompilerParams(collective_id=0, has_side_effects=True,
                                             vmem_limit_bytes=60 << 20),
        name="class_pass",
    )(particles, references, shifts.T, rotation[None], owner.T, class_offset[None], ctf_group[None], ctf_table)
    return best[0], new


def solution(mesh):
    return jax.shard_map(
        per_device,
        mesh=mesh,
        in_specs=(
            P(("dom", "cls"), None),
            P("cls", "dom"),
            P(("dom", "cls"), None),
            P(("dom", "cls")),
            P(("dom", "cls")),
            P(("dom", "cls"), None),
            P(("dom", "cls")),
            P(),
        ),
        out_specs=(P(("dom", "cls")), P("cls", "dom")),
        check_vma=False,
    )
```

```python
import math

import jax
import jax.numpy as jnp
from jax import lax
from jax.experimental import pallas as pl
from jax.experimental.pallas import tpu as pltpu
from jax.sharding import PartitionSpec as P

BOX = 128
SPAN = 16
EARLY = -0.5
tau_reg = 1.0
ROWS = 16
F32 = jnp.float32
BF16 = jnp.bfloat16
MESH = pl.DeviceIdType.MESH


def split_angles(angles):
    even = angles & -angles
    return even, angles // even


def lin(terms):
    total = None
    for factor, value in terms:
        if value is None or abs(factor) < 1e-12:
            continue
        if total is None:
            total = value if abs(factor - 1) < 1e-12 else (-value if abs(factor + 1) < 1e-12 else value * factor)
        elif abs(factor - 1) < 1e-12:
            total = total + value
        elif abs(factor + 1) < 1e-12:
            total = total - value
        else:
            total = total + value * factor
    return total


def add(a, b):
    return b if a is None else (a if b is None else a + b)


def sub(a, b):
    if b is None:
        return a
    return -b if a is None else a - b


def turn(re, im, part, whole):
    if part == 0:
        return re, im
    c, s = math.cos(2 * math.pi * part / whole), math.sin(2 * math.pi * part / whole)
    return lin([(c, re), (-s, im)]), lin([(s, re), (c, im)])


def three(a, b, c, sign):
    tr, ti = add(b[0], c[0]), add(b[1], c[1])
    er, ei = lin([(sign * math.sqrt(0.75), sub(b[0], c[0]))]), None
    if b[1] is not None or c[1] is not None:
        ei = lin([(sign * math.sqrt(0.75), sub(b[1], c[1]))])
    mr = sub(a[0], lin([(0.5, tr)]))
    mi = None if ti is None and a[1] is None else sub(a[1], lin([(0.5, ti)]))
    first = (add(a[0], tr), None if a[1] is None and ti is None else add(a[1], ti))
    second = (mr if ei is None else mr - ei, add(mi, er))
    third = (mr if ei is None else mr + ei, -er if mi is None else mi - er)
    return first, second, third


def nine_dft(values, sign, wanted):
    inner = [three(values[j], values[j + 3], values[j + 6], sign) for j in range(3)]
    out = {}
    for k in range(3):
        row = [turn(*inner[j][k], sign * j * k, 9) for j in range(3)]
        for l, x in enumerate(three(*row, sign)):
            out[k + 3 * l] = x
    return {k: out[k] for k in out if k in wanted}


def odd_dft(values, sign, wanted):
    n = len(values)
    if n == 9:
        return nine_dft(values, sign, wanted)
    half = n // 2
    sums = [(add(values[j][0], values[n - j][0]), add(values[j][1], values[n - j][1])) for j in range(1, half + 1)]
    diffs = [(sub(values[j][0], values[n - j][0]), sub(values[j][1], values[n - j][1])) for j in range(1, half + 1)]
    out = {}
    for k in range(half + 1):
        pair = [x for x in (k, n - k) if x in wanted]
        if not pair:
            continue
        cs = [math.cos(2 * math.pi * ((j * k) % n) / n) for j in range(1, half + 1)]
        sn = [sign * math.sin(2 * math.pi * ((j * k) % n) / n) for j in range(1, half + 1)]
        even_re = lin([(1.0, values[0][0])] + [(c, s[0]) for c, s in zip(cs, sums)])
        even_im = lin([(1.0, values[0][1])] + [(c, s[1]) for c, s in zip(cs, sums)])
        odd_re = lin([(-s, d[1]) for s, d in zip(sn, diffs)])
        odd_im = lin([(s, d[0]) for s, d in zip(sn, diffs)])
        for x in pair:
            if x == k:
                out[x] = (add(even_re, odd_re), add(even_im, odd_im))
            else:
                out[x] = (sub(even_re, odd_re), sub(even_im, odd_im))
    return out


def real_eight_dft(v):
    r = math.sqrt(0.5)
    s = [v[j] + v[j + 4] for j in range(4)]
    d = [v[j] - v[j + 4] for j in range(4)]
    a, b = s[0] + s[2], s[1] + s[3]
    p, q = r * (d[1] - d[3]), r * (d[1] + d[3])
    return [(a + b, None), (d[0] + p, -d[2] - q), (s[0] - s[2], s[3] - s[1]), (d[0] - p, d[2] - q), (a - b, None)]


def real_even_dft(values):
    n = len(values)
    if n == 8:
        return real_eight_dft(values)
    half = n // 2
    sums = [add(values[j], values[n - j]) for j in range(1, half)]
    diffs = [sub(values[j], values[n - j]) for j in range(1, half)]
    plus, minus = values[0] + values[half], values[0] - values[half]
    out = []
    for k in range(half + 1):
        cs = [math.cos(2 * math.pi * j * k / n) for j in range(1, half)]
        sn = [math.sin(2 * math.pi * j * k / n) for j in range(1, half)]
        re = lin([(1.0, minus if k % 2 else plus)] + list(zip(cs, sums)))
        im = lin([(-s, d) for s, d in zip(sn, diffs)]) if 0 < k < half else None
        out.append((re, im))
    return out


def forward_fft(load, store, angles):
    n1, n2 = split_angles(angles)
    inner = [real_even_dft([load(n2 * i + j) for i in range(n1)]) for j in range(n2)]
    for k1 in range(n1 // 2 + 1):
        values = [turn(*inner[j][k1], -((j * k1) % angles), angles) for j in range(n2)]
        for k2 in range(n2):
            pass
        wanted = set(range(n2)) if 0 < k1 < n1 // 2 else set(range(n2 // 2 + 1))
        for k2, (re, im) in odd_dft(values, -1.0, wanted).items():
            m = k1 + n1 * k2
            if m > angles // 2:
                m, im = angles - m, (None if im is None else -im)
            store(m, re, im)


def inverse_max(load, angles):
    n1, n2 = split_angles(angles)

    def value(m):
        if m == 0 or m == angles // 2:
            return load(m, 0), None
        if m > angles // 2:
            re, im = load(angles - m, 0), load(angles - m, 1)
            return re, -im
        return load(m, 0), load(m, 1)

    grid = []
    for k1 in range(n1 // 2 + 1):
        values = [value((k1 + n1 * k2) % angles) for k2 in range(n2)]
        got = odd_dft(values, 1.0, set(range(n2)))
        row = []
        for j in range(n2):
            row.append(turn(*got[j], (j * k1) % angles, angles))
        grid.append(row)
    best = None
    half = n1 // 2
    for j in range(n2):
        h0, h4 = grid[0][j][0], grid[half][j][0]
        if n1 == 8:
            r = math.sqrt(2.0)
            (a1, b1), (a2, b2), (a3, b3) = grid[1][j], grid[2][j], grid[3][j]
            plus, minus = h0 + h4, h0 - h4
            twice, sine = 2.0 * a2, 2.0 * b2
            w, e = r * (a1 - a3), r * (b1 + b3)
            tops = [plus + twice + 2.0 * jnp.abs(a1 + a3), plus - twice + 2.0 * jnp.abs(b1 - b3),
                    minus + w + jnp.abs(e + sine), minus - w + jnp.abs(e - sine)]
            for top in tops:
                best = top if best is None else jnp.maximum(best, top)
            continue
        plus, minus = h0 + h4, h0 - h4
        doubled = [(2.0 * grid[k][j][0], 2.0 * grid[k][j][1]) for k in range(1, half)]
        for i in range(half + 1):
            even = lin([(1.0, minus if i % 2 else plus)] + [(math.cos(2 * math.pi * i * (k + 1) / n1), doubled[k][0]) for k in range(half - 1)])
            odd = lin([(-math.sin(2 * math.pi * i * (k + 1) / n1), doubled[k][1]) for k in range(half - 1)]) if 0 < i < half else None
            top = even if odd is None else even + jnp.abs(odd)
            best = top if best is None else jnp.maximum(best, top)
    return best


def sin_cos_turns(u):
    u = u - jnp.floor(u + 0.5)
    v = (u * u) * (4 * math.pi * math.pi)
    s = jnp.full_like(v, 1.0 / math.factorial(17))
    for k in (15, 13, 11, 9, 7, 5, 3, 1):
        s = s * v + ((-1.0) ** (k // 2)) / math.factorial(k)
    c = jnp.full_like(v, -1.0 / math.factorial(18))
    for k in (16, 14, 12, 10, 8, 6, 4, 2, 0):
        c = c * v + ((-1.0) ** (k // 2)) / math.factorial(k)
    return s * (u * (2 * math.pi)), c


def fused(dims, part_hbm, refs_ref, shift_ref, turn_ref, owner_ref, offset_ref, group_ref, table_ref,
          best_ref, new_ref,
          part_ref, tab, phase, ctf_ref, rot_ref, meta_ref, buf, wch, ych, spec_p, spec_r, cross, contrib, got, metas, part, wpart, sbuf, rbuf, wrecv, sel_ref, keep, bsend, brecv, mid, mgot, jsend, jrecv,
          part_sem, own_sem, zsend, zrecv, psend, precv, csend, crecv, asend, arecv, msend, mrecv,
          ssend, srecv, wsend, wrecv_sem, xsend, xrecv):
    D, Z, angles, cyc = dims
    dom, zed = lax.axis_index("dom"), lax.axis_index("cls")
    rows, lanes = part_ref.shape[0], 2 * cyc
    local, width = refs_ref.shape
    pad = part.shape[1]
    bits = [1 << i for i in range(1, D.bit_length() - 1)]
    offsets = list(range(0, D, 2))
    paired = len(bits) == 2 and Z == 4
    parity = lax.rem(dom, 2)
    last, first = 2 + 2 * parity, 4 - 2 * parity
    along = [0, D - 2] if paired else [0]

    def to_dom(q):
        return {"dom": dom ^ q, "cls": zed}

    def to_cls(j):
        return {"dom": dom, "cls": lax.rem(zed + j, Z)}

    near_first = [sorted(range(Z), key=lambda o: (abs(o - z), o)) for z in range(Z)]
    origin = [sum(jnp.where(zed == z, near_first[z][k], 0) for z in range(Z)) for k in range(Z)]

    def remote(src, dst, s, r, where):
        return pltpu.make_async_remote_copy(src_ref=src, dst_ref=dst, send_sem=s, recv_sem=r,
                                            device_id=where, device_id_type=MESH)

    def block(q, o):
        return buf.at[dom ^ q, o]

    def z_copy(src, q, o, up):
        to = {"dom": dom, "cls": zed + 1 if up else zed - 1}
        line = along.index(q)
        return remote(src, buf.at[dom ^ q, o], zsend.at[1 if up else 0, line, o], zrecv.at[line, o], to)

    def z_pass(src, q, o, moving_up, moving_down):
        @pl.when(jnp.logical_and(moving_up, zed + 1 < Z))
        def _():
            z_copy(src, q, o, True).start()

        @pl.when(jnp.logical_and(moving_down, zed > 0))
        def _():
            z_copy(src, q, o, False).start()

    def source(q, o, h):
        return refs_ref if q == 0 and h == 0 else block(q, o)

    def plane_copy(child, bit, o, h):
        q = child ^ bit
        return remote(source(q, o, h), block(q, o), psend, precv.at[child // 2, o], to_dom(bit))

    def core_copy(q, o, h):
        return remote(source(q, o, h), block(q, o), csend, crecv.at[o], to_dom(1))

    def last_bit(q, h):
        return (1 << (q.bit_length() - 1)) if h % 2 == 0 else (q & -q)

    def at_hops(h, act):
        if h == 0:
            act(zed, 0)
            return
        for side in (1, -1):
            o = zed + side * h

            @pl.when(jnp.logical_and(o >= 0, o < Z))
            def _():
                act(o, side)

    fetch = pltpu.make_async_copy(part_hbm, part_ref, part_sem)
    fetch.start()
    barrier = pltpu.get_barrier_semaphore()
    for q in range(1, D):
        pl.semaphore_signal(barrier, inc=1, device_id=to_dom(q), device_id_type=MESH)
    for j in range(1, Z):
        pl.semaphore_signal(barrier, inc=1, device_id=to_cls(j), device_id_type=MESH)
    meta_ref[...] = jnp.zeros_like(meta_ref)
    meta_ref[pl.ds(0, 1), :] = owner_ref[...] * pad + offset_ref[...]
    meta_ref[pl.ds(1, 1), :] = group_ref[...]
    def column(row):
        return jnp.transpose(jnp.broadcast_to(row.astype(F32), (lanes, rows)))

    quarter, levels = angles // 4, tab.shape[1] // SPAN
    left = lax.broadcasted_iota(jnp.int32, (SPAN, lanes), 1) < cyc
    radius = (lax.rem(lax.broadcasted_iota(jnp.int32, (SPAN, lanes), 1), cyc) + 1).astype(F32) / BOX
    radius = radius * (lax.broadcasted_iota(jnp.int32, (SPAN, lanes), 0) - SPAN // 2).astype(F32)
    for a in range(quarter + 1):
        s, c = sin_cos_turns(radius * (math.cos(2 * math.pi * a / angles) if a < quarter else 0.0))
        for h, value in enumerate((c, jnp.where(left, -s, s))):
            for n in range(levels):
                tab[a, pl.ds(n * SPAN, SPAN), pl.ds(h * lanes, lanes)] = value.astype(BF16)
                value = value - value.astype(BF16).astype(F32)
    moved = jnp.concatenate([column(shift_ref[pl.ds(n, 1), :]) for n in range(2)], axis=0).astype(jnp.int32)
    steps = lax.rem(lax.broadcasted_iota(jnp.int32, (2 * rows, levels * SPAN), 1), SPAN) - SPAN // 2
    picked = jnp.where(moved[:, :levels * SPAN] == steps, 1.0, 0.0).astype(BF16)
    for a in range(quarter + 1):
        phase[a] = jnp.dot(picked, tab[a], preferred_element_type=F32)
    rot_ref[...] = column(turn_ref[...]).astype(jnp.int32)
    groups = table_ref.shape[0]
    table = table_ref[...]
    gcol = column(group_ref[...]).astype(jnp.int32)
    gcol = jnp.concatenate([gcol] * -(-groups // lanes), axis=1)[:, :groups]
    pick = jnp.where(gcol == lax.broadcasted_iota(jnp.int32, (rows, groups), 1), 1.0, 0.0)
    one = jnp.dot(pick, table, precision=lax.Precision.HIGHEST, preferred_element_type=F32)
    ctf_ref[...] = jnp.concatenate([one, one], axis=1)

    pl.semaphore_wait(barrier, D + Z - 2)

    own = pltpu.make_async_copy(refs_ref, buf.at[dom, zed], own_sem)
    own.start()
    z_pass(refs_ref, 0, zed, zed >= 0, zed >= 0)

    def children(q, h):
        return [(q ^ b, b) for b in bits if not q & b and last_bit(q ^ b, h) == b]

    def event(q, h, only=None):
        def act(o, side):
            if only == "plane":
                pass
            elif h and q in along:
                z_copy(refs_ref, q, o, True).wait_recv()
                if side < 0:
                    z_pass(block(q, o), q, o, zed >= 0, zed < 0)
                else:
                    z_pass(block(q, o), q, o, zed < 0, zed >= 0)
            elif q:
                plane_copy(q, last_bit(q, h), o, h).wait_recv()
                if q in along:
                    z_pass(block(q, o), q, o, zed >= 0, zed >= 0)
            if only == "line":
                return
            if not paired or q == 0:
                for child, b in children(q, h):
                    if not paired or child not in along:
                        plane_copy(child, b, o, h).start()
            elif h == 0 and q not in along:
                @pl.when(first == D - 2 - q)
                def _():
                    plane_copy(D - 2, D - 2 - q, o, h).start()
            core_copy(q, o, h).start()

        at_hops(h, act)

    event(0, 0)
    for q in range(1, D):
        remote(meta_ref, metas.at[q], msend, mrecv, to_dom(q)).start()
    metas[0] = meta_ref[...]

    plan = {("prep", 6): [(0, 1, "line"), (2, 0), (4, 0), (0, 1, "plane")]} if paired else {}

    def serve(*pairs):
        for q, h, *part_of in pairs:
            if h < Z:
                event(q, h, *part_of)

    fetch.wait()
    chunks = rows // ROWS
    low, high = split_angles(angles)

    def piece(ref, sl, a):
        if width % lanes == 0:
            return ref(a * lanes // width)[sl, pl.ds(a * lanes % width, lanes)]
        halves = [(a * lanes + h * cyc) for h in range(2)]
        return jnp.concatenate([ref(c // width)[sl, pl.ds(c % width, cyc)] for c in halves], axis=1)

    def twin_copy(i):
        start = pl.multiple_of(i * ROWS, ROWS)
        return remote(contrib.at[1, :, pl.ds(start, ROWS), :], contrib.at[0, :, pl.ds(rows + start, ROWS), :],
                      xsend, xrecv, to_dom(1))

    def prep_chunk(i, carry):
        sl = pl.ds(pl.multiple_of(i * ROWS, ROWS), ROWS)
        ctf = ctf_ref[sl, :]
        also = pl.ds(pl.multiple_of(rows + i * ROWS, ROWS), ROWS)

        def apply(a, c, s):
            for b, sign in ((a, 1), (a + angles // 2, -1)):
                x = part_ref[sl, pl.ds(b * lanes, lanes)].astype(F32)
                y = pltpu.roll(x, cyc, 1) * s
                wch[b] = (x * c + y if sign > 0 else x * c - y).astype(BF16)

        for a in range(quarter + 1):
            cx, sx = phase[a, sl, pl.ds(0, lanes)], phase[a, sl, pl.ds(lanes, lanes)]
            cy = phase[quarter - a, also, pl.ds(0, lanes)] * ctf
            sy = phase[quarter - a, also, pl.ds(lanes, lanes)] * ctf
            cc, ss, sc, cs = cx * cy, sx * sy, sx * cy, cx * sy
            apply(a, cc - ss, sc + cs)
            if 0 < a < quarter:
                apply(angles // 2 - a, cc + ss, cs - sc)

        def store(m, re, im):
            first = re.astype(BF16)
            second = jnp.zeros_like(first) if im is None else im.astype(BF16)
            lower = pl.ds(pl.multiple_of(rows + i * ROWS, ROWS), ROWS)
            spec_p[m, sl, pl.ds(0, lanes)] = first
            spec_p[m, sl, pl.ds(lanes, lanes)] = second
            spec_p[m, lower, pl.ds(0, lanes)] = second
            spec_p[m, lower, pl.ds(lanes, lanes)] = -first

        forward_fft(lambda a: wch[a].astype(F32), store, angles)
        rot = rot_ref[sl, :]
        bits_on = [jnp.where((rot & (1 << n)) != 0, 1.0, 0.0).astype(BF16) > 0 for n in range((angles - 1).bit_length())]
        memo = {}

        def staged(level, a):
            a = a % angles
            if (level, a) not in memo:
                if level == 0:
                    memo[level, a] = wch[a]
                else:
                    step = 1 << (level - 1)
                    on = bits_on[level - 1]
                    memo[level, a] = jnp.where(on, staged(level - 1, a + step), staged(level - 1, a))
            return memo[level, a]

        levels = low.bit_length() - 1
        for a in range(angles):
            ych[a] = staged(levels, a)
        for r in range(low):
            line = [ych[r + low * j] for j in range(high)]
            for bit in range((high - 1).bit_length()):
                on = bits_on[levels + bit]
                line = [jnp.where(on, line[(j + (1 << bit)) % high], line[j]) for j in range(high)]
            for j in range(high):
                a = r + low * j
                value = line[j]
                if paired:
                    d = a * lanes // width
                    contrib[parity if d % 2 == 0 else 1 - parity, d // 2, sl, pl.ds(a * lanes % width, lanes)] = value
                elif width % lanes == 0:
                    contrib[a * lanes // width, sl, pl.ds(a * lanes % width, lanes)] = value
                else:
                    for h in range(2):
                        col = a * lanes + h * cyc
                        contrib[col // width, sl, pl.ds(col % width, cyc)] = value[:, h * cyc:(h + 1) * cyc]
        if paired:
            @pl.when(i > 0)
            def _():
                twin_copy(i - 1).start()
        for c in range(chunks):
            if ("prep", c) in plan:
                @pl.when(i == c)
                def _():
                    serve(*plan["prep", c])
        return carry

    lax.fori_loop(0, chunks, prep_chunk, 0)

    spans = [(0, width)]
    if width % lanes == 0 and width // lanes >= 3:
        n = width // lanes
        last_cut, next_cut = n - max(1, n // 9), n - max(1, n // 9) - max(1, 2 * n // 9)
        cuts = [0, 2 * next_cut // 3, next_cut, last_cut, n]
        spans = [(x * lanes, (y - x) * lanes) for x, y in zip(cuts[:-1], cuts[1:])]

    def contrib_copy(q, c):
        cols = pl.ds(*spans[c])
        return remote(contrib.at[dom ^ q, :, cols], got.at[q, :, cols], asend.at[q, c], arecv.at[q, c], to_dom(q))

    def half_copy(h, c):
        cols = pl.ds(*spans[c])
        return remote(bsend.at[h, :, :, cols], brecv.at[h, :, :, cols], asend.at[0, 0], arecv.at[h, c],
                      {"dom": dom ^ first, "cls": zed})

    def joined(c):
        cols = pl.ds(*spans[c])
        return remote(mid.at[:, :, cols], mgot.at[:, :, cols], jsend, jrecv.at[c], {"dom": dom ^ last, "cls": zed})

    if paired:
        twin_copy(chunks - 1).start()
    else:
        for c in range(len(spans)):
            for q in range(1, D):
                contrib_copy(q, c).start()
        got[0] = contrib[dom]

    others = metas.at[pl.ds(1, D - 1)]
    remote(others, others, msend, mrecv, to_dom(1)).wait()
    ids = lax.broadcasted_iota(jnp.int32, (Z * pad, rows), 0)
    gids = lax.broadcasted_iota(jnp.int32, (groups, rows), 0)
    sel_ref[...] = jnp.concatenate([jnp.where(ids == metas[d, pl.ds(0, 1), :], 1.0, 0.0).astype(BF16) for d in range(D)], axis=1)

    def sum_span(c, which=(0, 1, 2, 3)):
        start, size = spans[c]
        cols = pl.ds(start, size)
        for h, chip in enumerate((dom ^ first ^ last, dom ^ first, dom ^ last, dom)):
            if h not in which:
                continue
            sums = jnp.dot(sel_ref[:, pl.ds(0, 2 * rows)], contrib[0, chip // 2, :, cols], preferred_element_type=F32)
            sums = sums.reshape(Z, pad, size)[:, :local, :]
            if h < 2:
                bsend[h, :, :, cols] = sums.astype(BF16)
                half_copy(h, c).start()
            elif h == 2:
                keep[:, pl.ds(0, local), cols] = sums
            else:
                part[:, pl.ds(0, local), cols] = sums

    if paired:
        twin_all = remote(contrib.at[1, :, pl.ds(0, rows), :], contrib.at[0, :, pl.ds(rows, rows), :], xsend, xrecv, to_dom(1))
        twin_all.wait_recv()
        sum_span(0)
    gsel = jnp.concatenate([jnp.where(gids == metas[d, pl.ds(1, 1), :], 1.0, 0.0).astype(BF16) for d in range(D)], axis=1)
    counts = lax.dot_general(sel_ref[...], gsel, (((1,), (1,)), ((), ())), preferred_element_type=F32)
    wsum = jnp.dot(counts, table * table, precision=lax.Precision.HIGHEST, preferred_element_type=F32)
    wpart[...] = wsum.reshape(Z, pad, wsum.shape[1])

    def w_copy(j):
        return remote(wpart.at[lax.rem(zed + j, Z)], wrecv.at[j], wsend, wrecv_sem, to_cls(j))

    for j in range(1, Z):
        w_copy(j).start()

    def s_copy(j, c):
        cols = pl.ds(*spans[c])
        return remote(sbuf.at[lax.rem(zed + j, Z), :, cols], rbuf.at[j, :, cols], ssend, srecv.at[c], to_cls(j))

    def send_span(c):
        start, size = spans[c]
        cols = pl.ds(start, size)
        if paired:
            half_copy(1, c).wait_recv()
            joined(c).wait_recv()
            both = brecv[1, :, :, cols].astype(F32) + mgot[:, :, cols].astype(F32)
            part[:, pl.ds(0, local), cols] = part[:, pl.ds(0, local), cols] + both
        else:
            for q in range(1, D):
                contrib_copy(q, c).wait()
            sums = jnp.dot(sel_ref[...], got[:, :, cols].reshape(D * rows, size), preferred_element_type=F32)
            part[:, :, cols] = sums.reshape(Z, pad, size)
        sbuf[:, :, cols] = part[:, pl.ds(0, local), cols].astype(BF16)
        for h in reversed(range(1, Z)):
            at_hops(h, lambda o, side: s_copy(lax.rem(o - zed + Z, Z), c).start())

    if paired:
        serve((0, 2), (6, 0))
    own.wait()

    def ref_rows(z, slot, start, count):
        sl = pl.ds(start, count)
        out = pl.ds(start, count)

        def store(m, re, im):
            second = jnp.zeros_like(re) if im is None else im
            spec_r[m, slot, out, pl.ds(0, lanes)] = re.astype(BF16)
            spec_r[m, slot, out, pl.ds(lanes, lanes)] = second.astype(BF16)

        forward_fft(lambda a: piece(lambda d: buf.at[d, z], sl, a).astype(F32), store, angles)

    whole = local // ROWS
    rest = local % ROWS

    def pass_on(c):
        start, size = spans[c]
        cols = pl.ds(start, size)
        half_copy(0, c).wait_recv()
        mid[:, :, cols] = (keep[:, pl.ds(0, local), cols] + brecv[0, :, :, cols].astype(F32)).astype(BF16)
        joined(c).start()

    def ref_block(k):
        came = buf.at[pl.ds(0, D // 2), origin[k]]
        remote(came, came, csend, crecv.at[origin[k]], to_dom(1)).wait_recv()

        def ref_step(n, carry):
            ref_rows(origin[k], k, pl.multiple_of(n * ROWS, ROWS), ROWS)
            return carry

        lax.fori_loop(0, whole, ref_step, 0)
        if rest:
            ref_rows(origin[k], k, whole * ROWS, rest)

    freqs = angles // 2 + 1
    groups_of = -(-local // 8)
    group = 4
    pieces = freqs // group

    def cross_step(m, lo, hi):
        lhs = spec_r[m, pl.ds(lo, hi - lo)].reshape((hi - lo) * pad, 2 * lanes)
        cross[m, pl.ds(lo * pad, (hi - lo) * pad), :] = lax.dot_general(
            lhs, spec_p[m], (((1,), (1,)), ((), ())), preferred_element_type=F32)

    def crosses(start, end, lo, hi):
        def step(n, carry):
            for g in range(group):
                cross_step(n * group + g, lo, hi)
            return carry

        lax.fori_loop(start, min(end, pieces), step, 0)
        if end > pieces:
            for m in range(pieces * group, freqs):
                cross_step(m, lo, hi)

    def back_step(n, best):
        z, j = n // groups_of, n % groups_of
        start = pl.multiple_of(z * pad + j * 8, 8)

        def load(m, p):
            return cross[m, pl.ds(start, 8), pl.ds(p * rows, rows)]

        top = inverse_max(load, angles)
        row = lax.broadcasted_iota(jnp.int32, (8, rows), 0) + j * 8
        return jnp.maximum(best, jnp.where(row < local, top, -jnp.inf))

    def backs(start, end, best):
        return lax.fori_loop(start, end, back_step, best)

    best = jnp.full((8, rows), -jnp.inf, F32)
    if paired:
        mid_z, all_z = Z // 2, Z * groups_of
        most = mid_z * groups_of
        ref_block(0)
        serve((2, 1), (4, 1))
        sum_span(1, (0, 2, 3))
        serve((0, 3))
        pass_on(0)
        for c in range(2, len(spans)):
            sum_span(c, (0,))
        sum_span(1, (1,))
        for c in range(2, len(spans)):
            sum_span(c, (1, 2, 3))
        serve((6, 1))
        ref_block(1)
        crosses(0, pieces + 1, 0, mid_z)
        serve((2, 2), (4, 2), (6, 2))
        send_span(0)
        pass_on(1)
        ref_block(2)
        best = backs(0, most // 2, best)
        pass_on(2)
        best = backs(most // 2, most, best)
        pass_on(3)
        serve(*[(q, 3) for q in (2, 4, 6)])
        send_span(1)
        ref_block(Z - 1)
        crosses(0, pieces // 2, mid_z, Z)
        send_span(2)
        crosses(pieces // 2, 3 * pieces // 4, mid_z, Z)
        send_span(3)
        crosses(3 * pieces // 4, pieces + 1, mid_z, Z)
        best = backs(most, all_z, best)
    else:
        for k in range(Z):
            serve(*sorted([(q, k) for q in offsets if q or k], key=lambda e: bin(e[0]).count("1")))
            ref_block(k)
        crosses(0, pieces + 1, 0, Z)
        best = backs(0, Z * groups_of, best)
        for c in range(len(spans)):
            send_span(c)
    best_ref[...] = jnp.max(best, axis=0, keepdims=True) * (1.0 / angles)

    weight = wpart[zed][:local, :]
    w_all = wrecv.at[pl.ds(1, Z - 1)]
    remote(w_all, w_all, wsend, wrecv_sem, to_cls(1)).wait()
    for j in range(1, Z):
        weight = weight + wrecv[j][:local, :]
    scale = 1.0 / (jnp.concatenate([weight, weight], axis=1) + tau_reg)
    for c, (start, size) in enumerate(spans):
        cols = pl.ds(start, size)
        total = part[zed, :, cols][:local, :]
        got_all = rbuf.at[pl.ds(1, Z - 1), :, cols]
        remote(got_all, got_all, ssend, srecv.at[c], to_cls(1)).wait_recv()
        for j in range(1, Z):
            total = total + rbuf[j, :, cols].astype(F32)
        new_ref[:, cols] = total * jnp.concatenate([scale] * -(-size // lanes), axis=1)[:, :size]

    remote(sbuf.at[pl.ds(0, Z - 1)], sbuf.at[pl.ds(0, Z - 1)], ssend, srecv.at[0], to_cls(1)).wait_send()
    if paired:
        remote(mid, mgot, jsend, jrecv.at[0], to_dom(1)).wait_send()
        remote(bsend, brecv, asend.at[0, 0], arecv.at[0, 0], to_dom(1)).wait_send()
        twin_all.wait_send()
    for q in along:
        for o in range(Z):
            @pl.when(jnp.logical_and(o <= zed, zed + 1 < Z))
            def _():
                z_copy(refs_ref, q, o, True).wait_send()

            @pl.when(jnp.logical_and(o >= zed, zed > 0))
            def _():
                z_copy(refs_ref, q, o, False).wait_send()
    remote(buf.at[pl.ds(0, D // 2)], buf.at[pl.ds(0, D // 2)], csend, crecv.at[0], to_dom(1)).wait_send()
    sent = buf.at[pl.ds(0, 3), pl.ds(0, 3)] if paired else buf.at[pl.ds(0, D // 2 - 1)]
    remote(sent, sent, psend, precv.at[0, 0], to_dom(2)).wait_send()


def per_device(particles, references, owner, class_offset, rotation, shifts, ctf_group, ctf_table):
    D, Z = lax.axis_size("dom"), lax.axis_size("cls")
    groups, cyc = ctf_table.shape
    rows, full = particles.shape
    lanes = 2 * cyc
    angles = full // lanes
    local, width = references.shape
    pad = -(-local // ROWS) * ROWS
    freqs = angles // 2 + 1
    chunks = 4
    dma = pltpu.SemaphoreType.DMA
    paired = D == 8 and Z == 4
    best, new = pl.pallas_call(
        lambda *refs: fused((D, Z, angles, cyc), *refs),
        out_shape=(pltpu.VMEM((1, rows), F32), pltpu.VMEM((local, width), F32)),
        in_specs=[pl.BlockSpec(memory_space=pl.ANY)] * 2 + [pl.BlockSpec(memory_space=pltpu.VMEM)] * 6,
        out_specs=[pl.BlockSpec(memory_space=pltpu.VMEM)] * 2,
        scratch_shapes=[
            pltpu.VMEM((rows, full), BF16),
            pltpu.VMEM((angles // 4 + 1, 3 * SPAN, 2 * lanes), BF16),
            pltpu.VMEM((angles // 4 + 1, 2 * rows, 2 * lanes), F32),
            pltpu.VMEM((rows, lanes), F32),
            pltpu.VMEM((rows, lanes), jnp.int32),
            pltpu.VMEM((8, rows), jnp.int32),
            pltpu.VMEM((D, Z, local, width), BF16),
            pltpu.VMEM((angles, ROWS, lanes), BF16),
            pltpu.VMEM((angles, ROWS, lanes), BF16),
            pltpu.VMEM((freqs, 2 * rows, 2 * lanes), BF16),
            pltpu.VMEM((freqs, Z, pad, 2 * lanes), BF16),
            pltpu.VMEM((freqs, Z * pad, 2 * rows), F32),
            pltpu.VMEM((2, D // 2, 2 * rows, width) if paired else (D, rows, width), BF16),
            pltpu.VMEM((1, ROWS, lanes) if paired else (D, rows, width), BF16),
            pltpu.VMEM((D, 8, rows), jnp.int32),
            pltpu.VMEM((Z, pad, width), F32),
            pltpu.VMEM((Z, pad, cyc), F32),
            pltpu.VMEM((Z, local, width), BF16),
            pltpu.VMEM((Z, local, width), BF16),
            pltpu.VMEM((Z, pad, cyc), F32),
            pltpu.VMEM((Z * pad, D * rows), BF16),
            pltpu.VMEM((Z, pad, width) if paired else (1, 8, lanes), F32),
            pltpu.VMEM((2, Z, local, width) if paired else (1, 1, ROWS, lanes), BF16),
            pltpu.VMEM((2, Z, local, width) if paired else (1, 1, ROWS, lanes), BF16),
            pltpu.VMEM((Z, local, width), BF16),
            pltpu.VMEM((Z, local, width), BF16),
            dma, dma((chunks,)),
            dma, dma, dma((2, 2, Z)), dma((2, Z)),
            dma, dma((D // 2, Z)), dma, dma((Z,)),
            dma((1, 1) if paired else (D, chunks)), dma((2 if paired else D, chunks)), dma, dma,
            dma, dma((chunks,)), dma, dma, dma, dma,
        ],
        compiler_params=pltpu.CompilerParams(collective_id=0, has_side_effects=True,
                                             vmem_limit_bytes=60 << 20),
        name="class_pass",
    )(particles, references, shifts.T, rotation[None], owner.T, class_offset[None], ctf_group[None], ctf_table)
    return best[0], new


def solution(mesh):
    return jax.shard_map(
        per_device,
        mesh=mesh,
        in_specs=(
            P(("dom", "cls"), None),
            P("cls", "dom"),
            P(("dom", "cls"), None),
            P(("dom", "cls")),
            P(("dom", "cls")),
            P(("dom", "cls"), None),
            P(("dom", "cls")),
            P(),
        ),
        out_specs=(P(("dom", "cls")), P("cls", "dom")),
        check_vma=False,
    )
```

```python
import math

import jax
import jax.numpy as jnp
from jax import lax
from jax.experimental import pallas as pl
from jax.experimental.pallas import tpu as pltpu
from jax.sharding import PartitionSpec as P

BOX = 128
SPAN = 16
EARLY = -0.5
tau_reg = 1.0
ROWS = 16
F32 = jnp.float32
BF16 = jnp.bfloat16
MESH = pl.DeviceIdType.MESH


def split_angles(angles):
    even = angles & -angles
    return even, angles // even


def lin(terms):
    total = None
    for factor, value in terms:
        if value is None or abs(factor) < 1e-12:
            continue
        if total is None:
            total = value if abs(factor - 1) < 1e-12 else (-value if abs(factor + 1) < 1e-12 else value * factor)
        elif abs(factor - 1) < 1e-12:
            total = total + value
        elif abs(factor + 1) < 1e-12:
            total = total - value
        else:
            total = total + value * factor
    return total


def add(a, b):
    return b if a is None else (a if b is None else a + b)


def sub(a, b):
    if b is None:
        return a
    return -b if a is None else a - b


def turn(re, im, part, whole):
    if part == 0:
        return re, im
    c, s = math.cos(2 * math.pi * part / whole), math.sin(2 * math.pi * part / whole)
    return lin([(c, re), (-s, im)]), lin([(s, re), (c, im)])


def three(a, b, c, sign):
    tr, ti = add(b[0], c[0]), add(b[1], c[1])
    er, ei = lin([(sign * math.sqrt(0.75), sub(b[0], c[0]))]), None
    if b[1] is not None or c[1] is not None:
        ei = lin([(sign * math.sqrt(0.75), sub(b[1], c[1]))])
    mr = sub(a[0], lin([(0.5, tr)]))
    mi = None if ti is None and a[1] is None else sub(a[1], lin([(0.5, ti)]))
    first = (add(a[0], tr), None if a[1] is None and ti is None else add(a[1], ti))
    second = (mr if ei is None else mr - ei, add(mi, er))
    third = (mr if ei is None else mr + ei, -er if mi is None else mi - er)
    return first, second, third


def nine_dft(values, sign, wanted):
    inner = [three(values[j], values[j + 3], values[j + 6], sign) for j in range(3)]
    out = {}
    for k in range(3):
        row = [turn(*inner[j][k], sign * j * k, 9) for j in range(3)]
        for l, x in enumerate(three(*row, sign)):
            out[k + 3 * l] = x
    return {k: out[k] for k in out if k in wanted}


def odd_dft(values, sign, wanted):
    n = len(values)
    if n == 9:
        return nine_dft(values, sign, wanted)
    half = n // 2
    sums = [(add(values[j][0], values[n - j][0]), add(values[j][1], values[n - j][1])) for j in range(1, half + 1)]
    diffs = [(sub(values[j][0], values[n - j][0]), sub(values[j][1], values[n - j][1])) for j in range(1, half + 1)]
    out = {}
    for k in range(half + 1):
        pair = [x for x in (k, n - k) if x in wanted]
        if not pair:
            continue
        cs = [math.cos(2 * math.pi * ((j * k) % n) / n) for j in range(1, half + 1)]
        sn = [sign * math.sin(2 * math.pi * ((j * k) % n) / n) for j in range(1, half + 1)]
        even_re = lin([(1.0, values[0][0])] + [(c, s[0]) for c, s in zip(cs, sums)])
        even_im = lin([(1.0, values[0][1])] + [(c, s[1]) for c, s in zip(cs, sums)])
        odd_re = lin([(-s, d[1]) for s, d in zip(sn, diffs)])
        odd_im = lin([(s, d[0]) for s, d in zip(sn, diffs)])
        for x in pair:
            if x == k:
                out[x] = (add(even_re, odd_re), add(even_im, odd_im))
            else:
                out[x] = (sub(even_re, odd_re), sub(even_im, odd_im))
    return out


def real_eight_dft(v):
    r = math.sqrt(0.5)
    s = [v[j] + v[j + 4] for j in range(4)]
    d = [v[j] - v[j + 4] for j in range(4)]
    a, b = s[0] + s[2], s[1] + s[3]
    p, q = r * (d[1] - d[3]), r * (d[1] + d[3])
    return [(a + b, None), (d[0] + p, -d[2] - q), (s[0] - s[2], s[3] - s[1]), (d[0] - p, d[2] - q), (a - b, None)]


def real_even_dft(values):
    n = len(values)
    if n == 8:
        return real_eight_dft(values)
    half = n // 2
    sums = [add(values[j], values[n - j]) for j in range(1, half)]
    diffs = [sub(values[j], values[n - j]) for j in range(1, half)]
    plus, minus = values[0] + values[half], values[0] - values[half]
    out = []
    for k in range(half + 1):
        cs = [math.cos(2 * math.pi * j * k / n) for j in range(1, half)]
        sn = [math.sin(2 * math.pi * j * k / n) for j in range(1, half)]
        re = lin([(1.0, minus if k % 2 else plus)] + list(zip(cs, sums)))
        im = lin([(-s, d) for s, d in zip(sn, diffs)]) if 0 < k < half else None
        out.append((re, im))
    return out


def forward_fft(load, store, angles):
    n1, n2 = split_angles(angles)
    inner = [real_even_dft([load(n2 * i + j) for i in range(n1)]) for j in range(n2)]
    for k1 in range(n1 // 2 + 1):
        values = [turn(*inner[j][k1], -((j * k1) % angles), angles) for j in range(n2)]
        for k2 in range(n2):
            pass
        wanted = set(range(n2)) if 0 < k1 < n1 // 2 else set(range(n2 // 2 + 1))
        for k2, (re, im) in odd_dft(values, -1.0, wanted).items():
            m = k1 + n1 * k2
            if m > angles // 2:
                m, im = angles - m, (None if im is None else -im)
            store(m, re, im)


def inverse_max(load, angles):
    n1, n2 = split_angles(angles)

    def value(m):
        if m == 0 or m == angles // 2:
            return load(m, 0), None
        if m > angles // 2:
            re, im = load(angles - m, 0), load(angles - m, 1)
            return re, -im
        return load(m, 0), load(m, 1)

    grid = []
    for k1 in range(n1 // 2 + 1):
        values = [value((k1 + n1 * k2) % angles) for k2 in range(n2)]
        got = odd_dft(values, 1.0, set(range(n2)))
        row = []
        for j in range(n2):
            row.append(turn(*got[j], (j * k1) % angles, angles))
        grid.append(row)
    best = None
    half = n1 // 2
    for j in range(n2):
        h0, h4 = grid[0][j][0], grid[half][j][0]
        if n1 == 8:
            r = math.sqrt(2.0)
            (a1, b1), (a2, b2), (a3, b3) = grid[1][j], grid[2][j], grid[3][j]
            plus, minus = h0 + h4, h0 - h4
            twice, sine = 2.0 * a2, 2.0 * b2
            w, e = r * (a1 - a3), r * (b1 + b3)
            tops = [plus + twice + 2.0 * jnp.abs(a1 + a3), plus - twice + 2.0 * jnp.abs(b1 - b3),
                    minus + w + jnp.abs(e + sine), minus - w + jnp.abs(e - sine)]
            for top in tops:
                best = top if best is None else jnp.maximum(best, top)
            continue
        plus, minus = h0 + h4, h0 - h4
        doubled = [(2.0 * grid[k][j][0], 2.0 * grid[k][j][1]) for k in range(1, half)]
        for i in range(half + 1):
            even = lin([(1.0, minus if i % 2 else plus)] + [(math.cos(2 * math.pi * i * (k + 1) / n1), doubled[k][0]) for k in range(half - 1)])
            odd = lin([(-math.sin(2 * math.pi * i * (k + 1) / n1), doubled[k][1]) for k in range(half - 1)]) if 0 < i < half else None
            top = even if odd is None else even + jnp.abs(odd)
            best = top if best is None else jnp.maximum(best, top)
    return best


def sin_cos_turns(u):
    u = u - jnp.floor(u + 0.5)
    v = (u * u) * (4 * math.pi * math.pi)
    s = jnp.full_like(v, 1.0 / math.factorial(17))
    for k in (15, 13, 11, 9, 7, 5, 3, 1):
        s = s * v + ((-1.0) ** (k // 2)) / math.factorial(k)
    c = jnp.full_like(v, -1.0 / math.factorial(18))
    for k in (16, 14, 12, 10, 8, 6, 4, 2, 0):
        c = c * v + ((-1.0) ** (k // 2)) / math.factorial(k)
    return s * (u * (2 * math.pi)), c


def fused(dims, part_hbm, refs_ref, shift_ref, turn_ref, owner_ref, offset_ref, group_ref, table_ref,
          best_ref, new_ref,
          part_ref, tab, phase, ctf_ref, rot_ref, meta_ref, buf, wch, ych, spec_p, spec_r, cross, contrib, got, metas, part, wpart, sbuf, rbuf, wrecv, sel_ref, keep, bsend, brecv, mid, mgot, jsend, jrecv,
          part_sem, own_sem, zsend, zrecv, psend, precv, csend, crecv, asend, arecv, msend, mrecv,
          ssend, srecv, wsend, wrecv_sem, xsend, xrecv):
    D, Z, angles, cyc = dims
    dom, zed = lax.axis_index("dom"), lax.axis_index("cls")
    rows, lanes = part_ref.shape[0], 2 * cyc
    local, width = refs_ref.shape
    pad = part.shape[1]
    bits = [1 << i for i in range(1, D.bit_length() - 1)]
    offsets = list(range(0, D, 2))
    paired = len(bits) == 2 and Z == 4
    parity = lax.rem(dom, 2)
    last, first = 2 + 2 * parity, 4 - 2 * parity
    along = [0, D - 2] if paired else [0]

    def to_dom(q):
        return {"dom": dom ^ q, "cls": zed}

    def to_cls(j):
        return {"dom": dom, "cls": lax.rem(zed + j, Z)}

    near_first = [sorted(range(Z), key=lambda o: (abs(o - z), o)) for z in range(Z)]
    origin = [sum(jnp.where(zed == z, near_first[z][k], 0) for z in range(Z)) for k in range(Z)]

    def remote(src, dst, s, r, where):
        return pltpu.make_async_remote_copy(src_ref=src, dst_ref=dst, send_sem=s, recv_sem=r,
                                            device_id=where, device_id_type=MESH)

    def block(q, o):
        return buf.at[dom ^ q, o]

    def z_copy(src, q, o, up):
        to = {"dom": dom, "cls": zed + 1 if up else zed - 1}
        line = along.index(q)
        return remote(src, buf.at[dom ^ q, o], zsend.at[1 if up else 0, line, o], zrecv.at[line, o], to)

    def z_pass(src, q, o, moving_up, moving_down):
        @pl.when(jnp.logical_and(moving_up, zed + 1 < Z))
        def _():
            z_copy(src, q, o, True).start()

        @pl.when(jnp.logical_and(moving_down, zed > 0))
        def _():
            z_copy(src, q, o, False).start()

    def source(q, o, h):
        return refs_ref if q == 0 and h == 0 else block(q, o)

    def plane_copy(child, bit, o, h):
        q = child ^ bit
        return remote(source(q, o, h), block(q, o), psend, precv.at[child // 2, o], to_dom(bit))

    def core_copy(q, o, h):
        return remote(source(q, o, h), block(q, o), csend, crecv.at[o], to_dom(1))

    def last_bit(q, h):
        return (1 << (q.bit_length() - 1)) if h % 2 == 0 else (q & -q)

    def at_hops(h, act):
        if h == 0:
            act(zed, 0)
            return
        for side in (1, -1):
            o = zed + side * h

            @pl.when(jnp.logical_and(o >= 0, o < Z))
            def _():
                act(o, side)

    fetch = pltpu.make_async_copy(part_hbm, part_ref, part_sem)
    fetch.start()
    barrier = pltpu.get_barrier_semaphore()
    for q in range(1, D):
        pl.semaphore_signal(barrier, inc=1, device_id=to_dom(q), device_id_type=MESH)
    for j in range(1, Z):
        pl.semaphore_signal(barrier, inc=1, device_id=to_cls(j), device_id_type=MESH)
    meta_ref[...] = jnp.zeros_like(meta_ref)
    meta_ref[pl.ds(0, 1), :] = owner_ref[...] * pad + offset_ref[...]
    meta_ref[pl.ds(1, 1), :] = group_ref[...]
    def column(row):
        return jnp.transpose(jnp.broadcast_to(row.astype(F32), (lanes, rows)))

    quarter, levels = angles // 4, tab.shape[1] // SPAN
    left = lax.broadcasted_iota(jnp.int32, (SPAN, lanes), 1) < cyc
    radius = (lax.rem(lax.broadcasted_iota(jnp.int32, (SPAN, lanes), 1), cyc) + 1).astype(F32) / BOX
    radius = radius * (lax.broadcasted_iota(jnp.int32, (SPAN, lanes), 0) - SPAN // 2).astype(F32)
    for a in range(quarter + 1):
        s, c = sin_cos_turns(radius * (math.cos(2 * math.pi * a / angles) if a < quarter else 0.0))
        for h, value in enumerate((c, jnp.where(left, -s, s))):
            for n in range(levels):
                tab[a, pl.ds(n * SPAN, SPAN), pl.ds(h * lanes, lanes)] = value.astype(BF16)
                value = value - value.astype(BF16).astype(F32)
    moved = jnp.concatenate([column(shift_ref[pl.ds(n, 1), :]) for n in range(2)], axis=0).astype(jnp.int32)
    steps = lax.rem(lax.broadcasted_iota(jnp.int32, (2 * rows, levels * SPAN), 1), SPAN) - SPAN // 2
    picked = jnp.where(moved[:, :levels * SPAN] == steps, 1.0, 0.0).astype(BF16)
    for a in range(quarter + 1):
        phase[a] = jnp.dot(picked, tab[a], preferred_element_type=F32)
    rot_ref[...] = column(turn_ref[...]).astype(jnp.int32)
    groups = table_ref.shape[0]
    table = table_ref[...]
    gcol = column(group_ref[...]).astype(jnp.int32)
    gcol = jnp.concatenate([gcol] * -(-groups // lanes), axis=1)[:, :groups]
    pick = jnp.where(gcol == lax.broadcasted_iota(jnp.int32, (rows, groups), 1), 1.0, 0.0)
    one = jnp.dot(pick, table, precision=lax.Precision.HIGHEST, preferred_element_type=F32)
    ctf_ref[...] = jnp.concatenate([one, one], axis=1)

    pl.semaphore_wait(barrier, D + Z - 2)

    own = pltpu.make_async_copy(refs_ref, buf.at[dom, zed], own_sem)
    own.start()
    z_pass(refs_ref, 0, zed, zed >= 0, zed >= 0)

    def children(q, h):
        return [(q ^ b, b) for b in bits if not q & b and last_bit(q ^ b, h) == b]

    def event(q, h, only=None):
        def act(o, side):
            if only == "plane":
                pass
            elif h and q in along:
                z_copy(refs_ref, q, o, True).wait_recv()
                if side < 0:
                    z_pass(block(q, o), q, o, zed >= 0, zed < 0)
                else:
                    z_pass(block(q, o), q, o, zed < 0, zed >= 0)
            elif q:
                plane_copy(q, last_bit(q, h), o, h).wait_recv()
                if q in along:
                    z_pass(block(q, o), q, o, zed >= 0, zed >= 0)
            if only == "line":
                return
            if not paired or q == 0:
                for child, b in children(q, h):
                    if not paired or child not in along:
                        plane_copy(child, b, o, h).start()
            elif h == 0 and q not in along:
                @pl.when(first == D - 2 - q)
                def _():
                    plane_copy(D - 2, D - 2 - q, o, h).start()
            core_copy(q, o, h).start()

        at_hops(h, act)

    event(0, 0)
    for q in range(1, D):
        remote(meta_ref, metas.at[q], msend, mrecv, to_dom(q)).start()
    metas[0] = meta_ref[...]

    plan = {("prep", 6): [(0, 1, "line"), (2, 0), (4, 0), (0, 1, "plane")]} if paired else {}

    def serve(*pairs):
        for q, h, *part_of in pairs:
            if h < Z:
                event(q, h, *part_of)

    fetch.wait()
    chunks = rows // ROWS
    low, high = split_angles(angles)

    def piece(ref, sl, a):
        if width % lanes == 0:
            return ref(a * lanes // width)[sl, pl.ds(a * lanes % width, lanes)]
        halves = [(a * lanes + h * cyc) for h in range(2)]
        return jnp.concatenate([ref(c // width)[sl, pl.ds(c % width, cyc)] for c in halves], axis=1)

    def twin_copy(i):
        start = pl.multiple_of(i * ROWS, ROWS)
        return remote(contrib.at[1, :, pl.ds(start, ROWS), :], contrib.at[0, :, pl.ds(rows + start, ROWS), :],
                      xsend, xrecv, to_dom(1))

    def prep_chunk(i, carry):
        sl = pl.ds(pl.multiple_of(i * ROWS, ROWS), ROWS)
        ctf = ctf_ref[sl, :]
        also = pl.ds(pl.multiple_of(rows + i * ROWS, ROWS), ROWS)

        def apply(a, c, s):
            for b, sign in ((a, 1), (a + angles // 2, -1)):
                x = part_ref[sl, pl.ds(b * lanes, lanes)].astype(F32)
                y = pltpu.roll(x, cyc, 1) * s
                wch[b] = (x * c + y if sign > 0 else x * c - y).astype(BF16)

        for a in range(quarter + 1):
            cx, sx = phase[a, sl, pl.ds(0, lanes)], phase[a, sl, pl.ds(lanes, lanes)]
            cy = phase[quarter - a, also, pl.ds(0, lanes)] * ctf
            sy = phase[quarter - a, also, pl.ds(lanes, lanes)] * ctf
            cc, ss, sc, cs = cx * cy, sx * sy, sx * cy, cx * sy
            apply(a, cc - ss, sc + cs)
            if 0 < a < quarter:
                apply(angles // 2 - a, cc + ss, cs - sc)

        def store(m, re, im):
            first = re.astype(BF16)
            second = jnp.zeros_like(first) if im is None else im.astype(BF16)
            lower = pl.ds(pl.multiple_of(rows + i * ROWS, ROWS), ROWS)
            spec_p[m, sl, pl.ds(0, lanes)] = first
            spec_p[m, sl, pl.ds(lanes, lanes)] = second
            spec_p[m, lower, pl.ds(0, lanes)] = second
            spec_p[m, lower, pl.ds(lanes, lanes)] = -first

        forward_fft(lambda a: wch[a].astype(F32), store, angles)
        rot = rot_ref[sl, :]
        bits_on = [jnp.where((rot & (1 << n)) != 0, 1.0, 0.0).astype(BF16) > 0 for n in range((angles - 1).bit_length())]
        memo = {}

        def staged(level, a):
            a = a % angles
            if (level, a) not in memo:
                if level == 0:
                    memo[level, a] = wch[a]
                else:
                    step = 1 << (level - 1)
                    on = bits_on[level - 1]
                    memo[level, a] = jnp.where(on, staged(level - 1, a + step), staged(level - 1, a))
            return memo[level, a]

        levels = low.bit_length() - 1
        for a in range(angles):
            ych[a] = staged(levels, a)
        for r in range(low):
            line = [ych[r + low * j] for j in range(high)]
            for bit in range((high - 1).bit_length()):
                on = bits_on[levels + bit]
                line = [jnp.where(on, line[(j + (1 << bit)) % high], line[j]) for j in range(high)]
            for j in range(high):
                a = r + low * j
                value = line[j]
                if paired:
                    d = a * lanes // width
                    contrib[parity if d % 2 == 0 else 1 - parity, d // 2, sl, pl.ds(a * lanes % width, lanes)] = value
                elif width % lanes == 0:
                    contrib[a * lanes // width, sl, pl.ds(a * lanes % width, lanes)] = value
                else:
                    for h in range(2):
                        col = a * lanes + h * cyc
                        contrib[col // width, sl, pl.ds(col % width, cyc)] = value[:, h * cyc:(h + 1) * cyc]
        if paired:
            @pl.when(i > 0)
            def _():
                twin_copy(i - 1).start()
        for c in range(chunks):
            if ("prep", c) in plan:
                @pl.when(i == c)
                def _():
                    serve(*plan["prep", c])
        return carry

    lax.fori_loop(0, chunks, prep_chunk, 0)

    spans = [(0, width)]
    if width % lanes == 0 and width // lanes >= 3:
        n = width // lanes
        last_cut, next_cut = n - max(1, n // 9), n - max(1, n // 9) - max(1, 2 * n // 9)
        cuts = [0, 2 * next_cut // 3, next_cut, last_cut, n]
        spans = [(x * lanes, (y - x) * lanes) for x, y in zip(cuts[:-1], cuts[1:])]

    def contrib_copy(q, c):
        cols = pl.ds(*spans[c])
        return remote(contrib.at[dom ^ q, :, cols], got.at[q, :, cols], asend.at[q, c], arecv.at[q, c], to_dom(q))

    def half_copy(h, c):
        cols = pl.ds(*spans[c])
        return remote(bsend.at[h, :, :, cols], brecv.at[h, :, :, cols], asend.at[0, 0], arecv.at[h, c],
                      {"dom": dom ^ first, "cls": zed})

    def joined(c):
        cols = pl.ds(*spans[c])
        return remote(mid.at[:, :, cols], mgot.at[:, :, cols], jsend, jrecv.at[c], {"dom": dom ^ last, "cls": zed})

    if paired:
        twin_copy(chunks - 1).start()
    else:
        for c in range(len(spans)):
            for q in range(1, D):
                contrib_copy(q, c).start()
        got[0] = contrib[dom]

    others = metas.at[pl.ds(1, D - 1)]
    remote(others, others, msend, mrecv, to_dom(1)).wait()
    ids = lax.broadcasted_iota(jnp.int32, (Z * pad, rows), 0)
    gids = lax.broadcasted_iota(jnp.int32, (groups, rows), 0)
    sel_ref[...] = jnp.concatenate([jnp.where(ids == metas[d, pl.ds(0, 1), :], 1.0, 0.0).astype(BF16) for d in range(D)], axis=1)

    def sum_span(c, which=(0, 1, 2, 3)):
        start, size = spans[c]
        cols = pl.ds(start, size)
        for h, chip in enumerate((dom ^ first ^ last, dom ^ first, dom ^ last, dom)):
            if h not in which:
                continue
            sums = jnp.dot(sel_ref[:, pl.ds(0, 2 * rows)], contrib[0, chip // 2, :, cols], preferred_element_type=F32)
            sums = sums.reshape(Z, pad, size)[:, :local, :]
            if h < 2:
                bsend[h, :, :, cols] = sums.astype(BF16)
                half_copy(h, c).start()
            elif h == 2:
                keep[:, pl.ds(0, local), cols] = sums
            else:
                part[:, pl.ds(0, local), cols] = sums

    if paired:
        twin_all = remote(contrib.at[1, :, pl.ds(0, rows), :], contrib.at[0, :, pl.ds(rows, rows), :], xsend, xrecv, to_dom(1))
        twin_all.wait_recv()
        sum_span(0)
    gsel = jnp.concatenate([jnp.where(gids == metas[d, pl.ds(1, 1), :], 1.0, 0.0).astype(BF16) for d in range(D)], axis=1)
    counts = lax.dot_general(sel_ref[...], gsel, (((1,), (1,)), ((), ())), preferred_element_type=F32)
    wsum = jnp.dot(counts, table * table, precision=lax.Precision.HIGHEST, preferred_element_type=F32)
    wpart[...] = wsum.reshape(Z, pad, wsum.shape[1])

    def w_copy(j):
        return remote(wpart.at[lax.rem(zed + j, Z)], wrecv.at[j], wsend, wrecv_sem, to_cls(j))

    for j in range(1, Z):
        w_copy(j).start()

    def s_copy(j, c):
        cols = pl.ds(*spans[c])
        return remote(sbuf.at[lax.rem(zed + j, Z), :, cols], rbuf.at[j, :, cols], ssend, srecv.at[c], to_cls(j))

    def send_span(c):
        start, size = spans[c]
        cols = pl.ds(start, size)
        if paired:
            half_copy(1, c).wait_recv()
            joined(c).wait_recv()
            both = brecv[1, :, :, cols].astype(F32) + mgot[:, :, cols].astype(F32)
            part[:, pl.ds(0, local), cols] = part[:, pl.ds(0, local), cols] + both
        else:
            for q in range(1, D):
                contrib_copy(q, c).wait()
            sums = jnp.dot(sel_ref[...], got[:, :, cols].reshape(D * rows, size), preferred_element_type=F32)
            part[:, :, cols] = sums.reshape(Z, pad, size)
        sbuf[:, :, cols] = part[:, pl.ds(0, local), cols].astype(BF16)
        for h in reversed(range(1, Z)):
            at_hops(h, lambda o, side: s_copy(lax.rem(o - zed + Z, Z), c).start())

    if paired:
        serve((0, 2), (6, 0))
    own.wait()

    def ref_rows(z, slot, start, count):
        sl = pl.ds(start, count)
        out = pl.ds(start, count)

        def store(m, re, im):
            second = jnp.zeros_like(re) if im is None else im
            spec_r[m, slot, out, pl.ds(0, lanes)] = re.astype(BF16)
            spec_r[m, slot, out, pl.ds(lanes, lanes)] = second.astype(BF16)

        forward_fft(lambda a: piece(lambda d: buf.at[d, z], sl, a).astype(F32), store, angles)

    whole = local // ROWS
    rest = local % ROWS

    def pass_on(c):
        start, size = spans[c]
        cols = pl.ds(start, size)
        half_copy(0, c).wait_recv()
        mid[:, :, cols] = (keep[:, pl.ds(0, local), cols] + brecv[0, :, :, cols].astype(F32)).astype(BF16)
        joined(c).start()

    def ref_block(k):
        came = buf.at[pl.ds(0, D // 2), origin[k]]
        remote(came, came, csend, crecv.at[origin[k]], to_dom(1)).wait_recv()

        def ref_step(n, carry):
            ref_rows(origin[k], k, pl.multiple_of(n * ROWS, ROWS), ROWS)
            return carry

        lax.fori_loop(0, whole, ref_step, 0)
        if rest:
            ref_rows(origin[k], k, whole * ROWS, rest)

    freqs = angles // 2 + 1
    groups_of = -(-local // 8)
    group = 4
    pieces = freqs // group

    def cross_step(m, lo, hi):
        lhs = spec_r[m, pl.ds(lo, hi - lo)].reshape((hi - lo) * pad, 2 * lanes)
        cross[m, pl.ds(lo * pad, (hi - lo) * pad), :] = lax.dot_general(
            lhs, spec_p[m], (((1,), (1,)), ((), ())), preferred_element_type=F32)

    def crosses(start, end, lo, hi):
        def step(n, carry):
            for g in range(group):
                cross_step(n * group + g, lo, hi)
            return carry

        lax.fori_loop(start, min(end, pieces), step, 0)
        if end > pieces:
            for m in range(pieces * group, freqs):
                cross_step(m, lo, hi)

    def back_step(n, best):
        z, j = n // groups_of, n % groups_of
        start = pl.multiple_of(z * pad + j * 8, 8)

        def load(m, p):
            return cross[m, pl.ds(start, 8), pl.ds(p * rows, rows)]

        top = inverse_max(load, angles)
        row = lax.broadcasted_iota(jnp.int32, (8, rows), 0) + j * 8
        return jnp.maximum(best, jnp.where(row < local, top, -jnp.inf))

    def backs(start, end, best):
        return lax.fori_loop(start, end, back_step, best)

    best = jnp.full((8, rows), -jnp.inf, F32)
    if paired:
        mid_z, all_z = Z // 2, Z * groups_of
        most = mid_z * groups_of
        ref_block(0)
        serve((2, 1), (4, 1))
        sum_span(1, (0, 2, 3))
        serve((0, 3))
        inner = jnp.logical_and(zed > 0, zed + 1 < Z)

        def serve_when(cond, *pairs):
            @pl.when(cond)
            def _():
                serve(*pairs)

        serve_when(inner, (6, 1))
        pass_on(0)
        for c in range(2, len(spans)):
            sum_span(c, (0,))
        sum_span(1, (1,))
        for c in range(2, len(spans)):
            sum_span(c, (1, 2, 3))
        serve_when(jnp.logical_not(inner), (6, 1))
        ref_block(1)
        crosses(0, pieces // 2, 0, mid_z)
        serve_when(inner, (6, 2))
        crosses(pieces // 2, pieces + 1, 0, mid_z)
        serve((2, 2), (4, 2))
        serve_when(jnp.logical_not(inner), (6, 2))
        pass_on(1)
        ref_block(2)
        send_span(0)
        best = backs(0, most // 2, best)
        pass_on(2)
        best = backs(most // 2, most, best)
        pass_on(3)
        send_span(1)
        serve(*[(q, 3) for q in (2, 4, 6)])
        ref_block(Z - 1)
        crosses(0, pieces // 2, mid_z, Z)
        send_span(2)
        crosses(pieces // 2, 3 * pieces // 4, mid_z, Z)
        send_span(3)
        crosses(3 * pieces // 4, pieces + 1, mid_z, Z)
        best = backs(most, all_z, best)
    else:
        for k in range(Z):
            serve(*sorted([(q, k) for q in offsets if q or k], key=lambda e: bin(e[0]).count("1")))
            ref_block(k)
        crosses(0, pieces + 1, 0, Z)
        best = backs(0, Z * groups_of, best)
        for c in range(len(spans)):
            send_span(c)
    best_ref[...] = jnp.max(best, axis=0, keepdims=True) * (1.0 / angles)

    weight = wpart[zed][:local, :]
    w_all = wrecv.at[pl.ds(1, Z - 1)]
    remote(w_all, w_all, wsend, wrecv_sem, to_cls(1)).wait()
    for j in range(1, Z):
        weight = weight + wrecv[j][:local, :]
    scale = 1.0 / (jnp.concatenate([weight, weight], axis=1) + tau_reg)
    for c, (start, size) in enumerate(spans):
        cols = pl.ds(start, size)
        total = part[zed, :, cols][:local, :]
        got_all = rbuf.at[pl.ds(1, Z - 1), :, cols]
        remote(got_all, got_all, ssend, srecv.at[c], to_cls(1)).wait_recv()
        for j in range(1, Z):
            total = total + rbuf[j, :, cols].astype(F32)
        new_ref[:, cols] = total * jnp.concatenate([scale] * -(-size // lanes), axis=1)[:, :size]

    remote(sbuf.at[pl.ds(0, Z - 1)], sbuf.at[pl.ds(0, Z - 1)], ssend, srecv.at[0], to_cls(1)).wait_send()
    if paired:
        remote(mid, mgot, jsend, jrecv.at[0], to_dom(1)).wait_send()
        remote(bsend, brecv, asend.at[0, 0], arecv.at[0, 0], to_dom(1)).wait_send()
        twin_all.wait_send()
    for q in along:
        for o in range(Z):
            @pl.when(jnp.logical_and(o <= zed, zed + 1 < Z))
            def _():
                z_copy(refs_ref, q, o, True).wait_send()

            @pl.when(jnp.logical_and(o >= zed, zed > 0))
            def _():
                z_copy(refs_ref, q, o, False).wait_send()
    remote(buf.at[pl.ds(0, D // 2)], buf.at[pl.ds(0, D // 2)], csend, crecv.at[0], to_dom(1)).wait_send()
    sent = buf.at[pl.ds(0, 3), pl.ds(0, 3)] if paired else buf.at[pl.ds(0, D // 2 - 1)]
    remote(sent, sent, psend, precv.at[0, 0], to_dom(2)).wait_send()


def per_device(particles, references, owner, class_offset, rotation, shifts, ctf_group, ctf_table):
    D, Z = lax.axis_size("dom"), lax.axis_size("cls")
    groups, cyc = ctf_table.shape
    rows, full = particles.shape
    lanes = 2 * cyc
    angles = full // lanes
    local, width = references.shape
    pad = -(-local // ROWS) * ROWS
    freqs = angles // 2 + 1
    chunks = 4
    dma = pltpu.SemaphoreType.DMA
    paired = D == 8 and Z == 4
    best, new = pl.pallas_call(
        lambda *refs: fused((D, Z, angles, cyc), *refs),
        out_shape=(pltpu.VMEM((1, rows), F32), pltpu.VMEM((local, width), F32)),
        in_specs=[pl.BlockSpec(memory_space=pl.ANY)] * 2 + [pl.BlockSpec(memory_space=pltpu.VMEM)] * 6,
        out_specs=[pl.BlockSpec(memory_space=pltpu.VMEM)] * 2,
        scratch_shapes=[
            pltpu.VMEM((rows, full), BF16),
            pltpu.VMEM((angles // 4 + 1, 3 * SPAN, 2 * lanes), BF16),
            pltpu.VMEM((angles // 4 + 1, 2 * rows, 2 * lanes), F32),
            pltpu.VMEM((rows, lanes), F32),
            pltpu.VMEM((rows, lanes), jnp.int32),
            pltpu.VMEM((8, rows), jnp.int32),
            pltpu.VMEM((D, Z, local, width), BF16),
            pltpu.VMEM((angles, ROWS, lanes), BF16),
            pltpu.VMEM((angles, ROWS, lanes), BF16),
            pltpu.VMEM((freqs, 2 * rows, 2 * lanes), BF16),
            pltpu.VMEM((freqs, Z, pad, 2 * lanes), BF16),
            pltpu.VMEM((freqs, Z * pad, 2 * rows), F32),
            pltpu.VMEM((2, D // 2, 2 * rows, width) if paired else (D, rows, width), BF16),
            pltpu.VMEM((1, ROWS, lanes) if paired else (D, rows, width), BF16),
            pltpu.VMEM((D, 8, rows), jnp.int32),
            pltpu.VMEM((Z, pad, width), F32),
            pltpu.VMEM((Z, pad, cyc), F32),
            pltpu.VMEM((Z, local, width), BF16),
            pltpu.VMEM((Z, local, width), BF16),
            pltpu.VMEM((Z, pad, cyc), F32),
            pltpu.VMEM((Z * pad, D * rows), BF16),
            pltpu.VMEM((Z, pad, width) if paired else (1, 8, lanes), F32),
            pltpu.VMEM((2, Z, local, width) if paired else (1, 1, ROWS, lanes), BF16),
            pltpu.VMEM((2, Z, local, width) if paired else (1, 1, ROWS, lanes), BF16),
            pltpu.VMEM((Z, local, width), BF16),
            pltpu.VMEM((Z, local, width), BF16),
            dma, dma((chunks,)),
            dma, dma, dma((2, 2, Z)), dma((2, Z)),
            dma, dma((D // 2, Z)), dma, dma((Z,)),
            dma((1, 1) if paired else (D, chunks)), dma((2 if paired else D, chunks)), dma, dma,
            dma, dma((chunks,)), dma, dma, dma, dma,
        ],
        compiler_params=pltpu.CompilerParams(collective_id=0, has_side_effects=True,
                                             vmem_limit_bytes=60 << 20),
        name="class_pass",
    )(particles, references, shifts.T, rotation[None], owner.T, class_offset[None], ctf_group[None], ctf_table)
    return best[0], new


def solution(mesh):
    return jax.shard_map(
        per_device,
        mesh=mesh,
        in_specs=(
            P(("dom", "cls"), None),
            P("cls", "dom"),
            P(("dom", "cls"), None),
            P(("dom", "cls")),
            P(("dom", "cls")),
            P(("dom", "cls"), None),
            P(("dom", "cls")),
            P(),
        ),
        out_specs=(P(("dom", "cls")), P("cls", "dom")),
        check_vma=False,
    )
```
